128 devices in a mesh: rep: 4 (over y_hi, core), fsdp: 32 (over x, z, y_lo).
Axes of the slice: x: 4, y: 4 (y_hi: 2, y_lo: 2; y = y_hi * 2 + y_lo), z: 4, core: 2. Of those that a mesh axis runs over, the one named last changes fastest.
Arguments:
- query_rows: bfloat16 [4, 12288, 2560], P('rep', 'fsdp'), may hold values from -5 to 5
- key_rows: bfloat16 [4, 12288, 2560], P('rep', 'fsdp'), may hold values from -5 to 5
- value_rows: bfloat16 [4, 12288, 2560], P('rep', 'fsdp'), may hold values from -5 to 5
- residual_in: bfloat16 [4, 12288, 2560], P('rep', 'fsdp'), may hold values from -6 to 6
- out_grad: bfloat16 [4, 12288, 2560], P('rep', 'fsdp'), may hold values from -6 to 6
- doc_ids: int32 [4, 12288], P('rep', 'fsdp'), may hold values from 0 to 191, never falling along the last dimension, each value on 1 to 256 neighbouring positions
- out_weight: bfloat16 [4, 2560, 2560], P('rep', 'fsdp'), may hold values from -0.125 to 0.125
- momentum: float32 [4, 2560, 2560], P('rep', 'fsdp'), may hold values from -192 to 192
- step_index: int32 [1], replicated, may hold values from 0 to 63
Outputs:
- block_out: bfloat16 [4, 12288, 2560], P('rep', 'fsdp')
- query_grad: bfloat16 [4, 12288, 2560], P('rep', 'fsdp')
- key_grad: bfloat16 [4, 12288, 2560], P('rep', 'fsdp')
- value_grad: bfloat16 [4, 12288, 2560], P('rep', 'fsdp')
- new_weight: bfloat16 [4, 2560, 2560], P('rep', 'fsdp')
- new_momentum: float32 [4, 2560, 2560], P('rep', 'fsdp')
The draws below stay inside these ranges and needn't reach their ends.
All inputs are finite; a program needn't handle non-finite values.
Results may differ from the reference program's by a relative error of at most 0.018.
Values may be sent and summed in bfloat16 or wider, within the bound.
No kernel may reach another device: no remote copies, remote signals or barrier semaphores. Data moves between devices by JAX's collectives and lax.ppermute only.
A program may use at most 192 MiB of HBM per device.

```python
import math
import jax
import jax.numpy as jnp
import numpy as np
from jax import lax

D = 2560
HEADS = 20
HEAD_SIZE = 128
TOK_DEV = 384
HD = 2560
TOKENS = 12288
N_REP = 4


def query_key_pair(key):
    shape = (N_REP, TOKENS, HD)
    first = jax.random.fold_in(key, 11)
    second = jax.random.fold_in(key, 12)
    queries = jnp.clip(jax.random.normal(first, shape, jnp.float32), -5.0, 5.0)
    keyset = jnp.clip(jax.random.normal(second, shape, jnp.float32), -5.0, 5.0)
    return (queries, keyset)


def draw_query_rows(key, part):
    return query_key_pair(key)[0].astype(jnp.bfloat16)


def draw_key_rows(key, part):
    return query_key_pair(key)[1].astype(jnp.bfloat16)


def block_scale(own_key, extent, split, least, top_value):
    def one(position, blocks):
        heights = jax.random.uniform(jax.random.fold_in(jax.random.fold_in(own_key, 6), position), (blocks,), jnp.float32, least / len(split), top_value / len(split))
        return jnp.repeat(jnp.exp(heights), extent[position] // blocks).reshape((-1,) + (1,) * (len(extent) - position - 1))

    gain = one(*split[0])
    for cut in split[1:]:
        gain = gain * one(*cut)
    return gain


def length_profile(count, total, reach, lean):
    portions = [(1 << 20) // math.isqrt(rank ** lean) + 1 for rank in range(2, count + 1)]
    surplus, counts = total - reach - (count - 1), [1] * (count - 1)
    while surplus > 0:
        free = [i for i in range(count - 1) if counts[i] < reach]
        pool, left = sum([portions[i] for i in free]), surplus
        for i in free:
            addition = min(reach - counts[i], max(1, left * portions[i] // pool), surplus)
            counts[i] = counts[i] + addition
            surplus = surplus - addition
    return np.array([reach] + counts)


def uneven_parts(own_key, count, total, most, lean):
    if count == 2:
        one = jax.random.randint(own_key, (), max(1, total - most), min(most, total - 1) + 1)
        return jnp.stack([one, total - one])
    sizes = jnp.asarray(length_profile(count, total, most, lean), jnp.int32)
    couples = (count - 1) // 2
    source_of, taker = sizes[1:1 + 2 * couples:2], sizes[2:2 + 2 * couples:2]
    slack = jnp.minimum(source_of - 1, most - taker)
    moved = jax.random.randint(jax.random.fold_in(own_key, 1), (couples,), 0, 1 << 20) % (slack + 1)
    sizes = sizes.at[1:1 + 2 * couples:2].set(source_of - moved).at[2:2 + 2 * couples:2].set(taker + moved)
    return sizes[jax.random.permutation(jax.random.fold_in(own_key, 2), count)]


def bell_draw(own_key, dims, deviation, most, cuts=(), kind=jnp.bfloat16):
    values = deviation * jax.random.normal(own_key, dims, jnp.float32)
    if cuts:
        values = values * block_scale(own_key, dims, cuts, -0.22, 0.18)
    return jnp.clip(values, -most, most).astype(kind)


def setup_inputs(seed: int = 0) -> dict:
    streams_of = jax.random.split(jax.random.key(seed), 10)
    query_rows = draw_query_rows(jax.random.fold_in(streams_of[9], 71), 0)
    key_rows = draw_key_rows(jax.random.fold_in(streams_of[9], 71), 0)
    value_rows = bell_draw(streams_of[2], (N_REP, TOKENS, HD), 1.0, 5.0, ((0, 4), (1, 32)))
    residual_in = bell_draw(streams_of[3], (N_REP, TOKENS, D), 1.0, 6.0, ((0, 4), (1, 32)))
    out_grad = bell_draw(streams_of[4], (N_REP, TOKENS, D), 1.0, 6.0, ((0, 4), (1, 32)))
    doc_ids = jax.vmap(lambda own: jnp.searchsorted(jnp.cumsum(uneven_parts(own, max(4, TOKENS // 64), TOKENS, min(256, TOKENS // 2), 1)), jnp.arange(TOKENS), side="right"))(jax.random.split(streams_of[5], N_REP)).reshape((N_REP, TOKENS)).astype(jnp.int32)
    out_weight = bell_draw(streams_of[6], (N_REP, HD, D), HD ** -0.5, 0.125, ((0, 4), (1, 32)))
    momentum = bell_draw(streams_of[7], (N_REP, HD, D), 32.0, 192.0, ((0, 4), (1, 32)), jnp.float32)
    step_index = jax.random.randint(streams_of[8], (1,), 0, 64).astype(jnp.int32)
    return {"query_rows": query_rows, "key_rows": key_rows, "value_rows": value_rows, "residual_in": residual_in, "out_grad": out_grad, "doc_ids": doc_ids, "out_weight": out_weight, "momentum": momentum, "step_index": step_index}


momentum_decay = 0.9
learning_rate = 0.0003


def rounded(values):
    return lax.optimization_barrier(values.astype(jnp.bfloat16)).astype(jnp.float32)


def attend(query_block, key_block, value_block, doc_block):
    length = query_block.shape[0]
    score_scale = HEAD_SIZE ** -0.5
    query_heads = query_block.astype(jnp.float32).reshape(length, HEADS, HEAD_SIZE)
    key_heads = key_block.astype(jnp.float32).reshape(length, HEADS, HEAD_SIZE)
    value_heads = value_block.astype(jnp.float32).reshape(length, HEADS, HEAD_SIZE)
    scores = jnp.einsum("qhd,khd->hqk", query_heads, key_heads) * score_scale
    places = jnp.arange(length, dtype=jnp.int32)
    allowed = (places[None, :] <= places[:, None]) & (doc_block[:, None] == doc_block[None, :])
    scores = jnp.where(allowed[None], scores, -jnp.inf)
    row_peaks = jnp.max(scores, axis=-1, keepdims=True)
    exponents = jnp.exp(scores - row_peaks)
    attn_probs = exponents / jnp.sum(exponents, axis=-1, keepdims=True)
    probs_low = rounded(attn_probs)
    context = jnp.einsum("hqk,khd->qhd", probs_low, value_heads)
    context = context.reshape(length, HEADS * HEAD_SIZE).astype(jnp.bfloat16)
    return context, attn_probs, probs_low, query_heads, key_heads, value_heads


def attend_back(context_grad, attn_probs, probs_low, query_heads, key_heads, value_heads):
    length = query_heads.shape[0]
    score_scale = HEAD_SIZE ** -0.5
    grad_heads = context_grad.astype(jnp.float32).reshape(length, HEADS, HEAD_SIZE)
    value_grad = jnp.einsum("hqk,qhd->khd", probs_low, grad_heads)
    prob_grad = jnp.einsum("qhd,khd->hqk", grad_heads, value_heads)
    row_delta = jnp.sum(prob_grad * attn_probs, axis=-1, keepdims=True)
    score_grad = rounded(attn_probs * (prob_grad - row_delta) * score_scale)
    query_grad = jnp.einsum("hqk,khd->qhd", score_grad, key_heads)
    key_grad = jnp.einsum("hqk,qhd->khd", score_grad, query_heads)
    width = HEADS * HEAD_SIZE
    return (query_grad.reshape(length, width).astype(jnp.bfloat16),
            key_grad.reshape(length, width).astype(jnp.bfloat16),
            value_grad.reshape(length, width).astype(jnp.bfloat16))


def reference(query_rows, key_rows, value_rows, residual_in, out_grad, doc_ids, out_weight, momentum, step_index):
    hidden = HEADS * HEAD_SIZE
    blocks = TOKENS // TOK_DEV
    outputs_block, outputs_query, outputs_key, outputs_value = [], [], [], []
    moments, stepped_all = [], []
    for replica in range(N_REP):
        weight = out_weight[replica]

        def one_block(running, pieces):
            query_block, key_block, value_block, resid_block, grad_block, doc_block = pieces
            context, attn_probs, probs_low, query_heads, key_heads, value_heads = attend(query_block, key_block, value_block, doc_block)
            projected = jnp.dot(context, weight, preferred_element_type=jnp.float32)
            block_out = (resid_block.astype(jnp.float32) + projected).astype(jnp.bfloat16)
            context_grad = lax.dot_general(grad_block, weight, (((1,), (1,)), ((), ())), preferred_element_type=jnp.float32).astype(jnp.bfloat16)
            query_grad, key_grad, value_grad = attend_back(context_grad, attn_probs, probs_low, query_heads, key_heads, value_heads)
            weight_term = lax.dot_general(context, grad_block, (((0,), (0,)), ((), ())), preferred_element_type=jnp.float32)
            return running + rounded(weight_term), (block_out, query_grad, key_grad, value_grad)

        def per_block(array):
            return array[replica].reshape((blocks, TOK_DEV) + array.shape[2:])

        pieces = (per_block(query_rows), per_block(key_rows), per_block(value_rows),
                  per_block(residual_in), per_block(out_grad), per_block(doc_ids))
        weight_grad, results = lax.scan(one_block, jnp.zeros((hidden, D), jnp.float32), pieces)
        outputs_block.append(results[0].reshape(TOKENS, D))
        outputs_query.append(results[1].reshape(TOKENS, hidden))
        outputs_key.append(results[2].reshape(TOKENS, hidden))
        outputs_value.append(results[3].reshape(TOKENS, hidden))
        new_momentum = momentum_decay * momentum[replica] + weight_grad
        moments.append(new_momentum)
        stepped_all.append((weight.astype(jnp.float32) - learning_rate * new_momentum).astype(jnp.bfloat16))
    stepped = jnp.stack(stepped_all)
    levels = N_REP.bit_length() - 1
    chosen_level = (step_index[0] % levels).astype(jnp.int32)
    partner = jnp.bitwise_xor(jnp.arange(N_REP, dtype=jnp.int32), jnp.left_shift(jnp.ones((), jnp.int32), chosen_level))
    new_weight = ((stepped.astype(jnp.float32) + stepped[partner].astype(jnp.float32)) * 0.5).astype(jnp.bfloat16)
    return (jnp.stack(outputs_block), jnp.stack(outputs_query), jnp.stack(outputs_key),
            jnp.stack(outputs_value), new_weight, jnp.stack(moments))
```

```python
import functools

import jax
import jax.numpy as jnp
from jax import lax
from jax.experimental import pallas as pl
from jax.experimental.pallas import tpu as pltpu
from jax.sharding import Mesh
from jax.sharding import PartitionSpec as P

HEADS = 20
HEAD_SIZE = 128
TOK = 384
WIDTH = 2560
SHARD = 80
AX, AZ, AY = "fsdp_0", "fsdp_1", "fsdp_2"
FSDP = (AX, AZ, AY)

momentum_decay = 0.9
learning_rate = 0.0003
score_scale = HEAD_SIZE ** (-0.5)

FORWARD_HEADS = 5
BACKWARD_HEADS = 2

bf16 = jnp.bfloat16
f32 = jnp.float32


def swapped(block, axis, distance):
    count = lax.axis_size(axis)
    return lax.ppermute(block, axis, [(i, i ^ (1 << distance)) for i in range(count)])


def dot(a, b, dims):
    return lax.dot_general(a, b, (dims, ((), ())), preferred_element_type=f32)


def mask_bias(doc_col, doc_row):
    rows = lax.broadcasted_iota(jnp.int32, (TOK, TOK), 0)
    cols = lax.broadcasted_iota(jnp.int32, (TOK, TOK), 1)
    allowed = (cols <= rows) & (doc_col == doc_row)
    return jnp.where(allowed, 0.0, -1e30).astype(f32)


def softmax_rows(q, k, bias):
    scores = dot(q, k, ((1,), (1,))) * score_scale + bias
    peak = jnp.max(scores, axis=-1, keepdims=True)
    e = jnp.exp(scores - peak)
    return e * (1.0 / jnp.sum(e, axis=-1, keepdims=True))


def forward_kernel(q, k, v, og, doc_col, doc_row, *refs):
    context, term, bias = refs[-3:]

    @pl.when(pl.program_id(0) == 0)
    def _():
        bias[...] = mask_bias(doc_col[:, :1], doc_row[:1, :])

    for h in range(FORWARD_HEADS):
        cols = slice(h * HEAD_SIZE, (h + 1) * HEAD_SIZE)
        probs = softmax_rows(q[:, cols], k[:, cols], bias[...])
        context[:, cols] = dot(probs.astype(bf16), v[:, cols], ((1,), (0,))).astype(bf16)
    term[...] = dot(context[...], og[...], ((0,), (0,))).astype(bf16)


def whole(shape):
    return pl.BlockSpec(shape, lambda i: (0, 0), pipeline_mode=pl.Buffered(1))


def forward_pass(q, k, v, og, doc_col, doc_row, first, count, earlier=()):
    size = FORWARD_HEADS * HEAD_SIZE
    column = pl.BlockSpec((TOK, size), lambda i: (0, i + first))
    return pl.pallas_call(
        forward_kernel,
        out_shape=[jax.ShapeDtypeStruct((TOK, WIDTH), bf16), jax.ShapeDtypeStruct((WIDTH, WIDTH), bf16)],
        grid_spec=pltpu.PrefetchScalarGridSpec(
            num_scalar_prefetch=0,
            grid=(count,),
            in_specs=[column, column, column, whole((TOK, WIDTH)), whole((TOK, HEAD_SIZE)), whole((8, TOK))]
            + [pl.BlockSpec(memory_space=pl.ANY)] * len(earlier),
            out_specs=[column, pl.BlockSpec((size, WIDTH), lambda i: (i + first, 0))],
            scratch_shapes=[pltpu.VMEM((TOK, TOK), f32)],
        ),
        input_output_aliases={6 + i: i for i in range(len(earlier))},
        compiler_params=pltpu.CompilerParams(
            dimension_semantics=("arbitrary",), vmem_limit_bytes=60 * 1024 * 1024
        ),
        cost_estimate=pl.CostEstimate(
            flops=int(1.65e9) * count, transcendentals=750000 * count, bytes_accessed=int(6e6) * count
        ),
        name="attend_forward",
    )(q, k, v, og, doc_col, doc_row, *earlier)


def backward_kernel(q, k, v, og, ctx, res, doc_col, doc_row, w_rows, w_cols, block_out, qg, kg, vg, bias):
    @pl.when(pl.program_id(0) == 0)
    def _():
        bias[...] = mask_bias(doc_col[:, :1], doc_row[:1, :])

    cg_all = dot(og[...], w_rows[...], ((1,), (1,))).astype(bf16)
    block_out[...] = (res[...].astype(f32) + dot(ctx[...], w_cols[...], ((1,), (0,)))).astype(bf16)
    for h in range(BACKWARD_HEADS):
        cols = slice(h * HEAD_SIZE, (h + 1) * HEAD_SIZE)
        qh, kh, vh, cg = q[:, cols], k[:, cols], v[:, cols], cg_all[:, cols]
        probs = softmax_rows(qh, kh, bias[...])
        vg[:, cols] = dot(probs.astype(bf16), cg, ((0,), (0,))).astype(bf16)
        pg = dot(cg, vh, ((1,), (1,)))
        delta = jnp.sum(pg * probs, axis=-1, keepdims=True)
        ds = (probs * (pg - delta) * score_scale).astype(bf16)
        qg[:, cols] = dot(ds, kh, ((1,), (0,))).astype(bf16)
        kg[:, cols] = dot(ds, qh, ((0,), (0,))).astype(bf16)


def backward_pass(q, k, v, og, ctx, res, doc_col, doc_row, weight):
    size = BACKWARD_HEADS * HEAD_SIZE
    column = pl.BlockSpec((TOK, size), lambda i: (0, i))
    return pl.pallas_call(
        backward_kernel,
        out_shape=[jax.ShapeDtypeStruct((TOK, WIDTH), bf16)] * 4,
        grid_spec=pltpu.PrefetchScalarGridSpec(
            num_scalar_prefetch=0,
            grid=(HEADS // BACKWARD_HEADS,),
            in_specs=[column, column, column, whole((TOK, WIDTH)), whole((TOK, WIDTH)), column]
            + [whole((TOK, HEAD_SIZE)), whole((8, TOK))]
            + [pl.BlockSpec((size, WIDTH), lambda i: (i, 0)), pl.BlockSpec((WIDTH, size), lambda i: (0, i))],
            out_specs=[column] * 4,
            scratch_shapes=[pltpu.VMEM((TOK, TOK), f32)],
        ),
        compiler_params=pltpu.CompilerParams(
            dimension_semantics=("arbitrary",), vmem_limit_bytes=60 * 1024 * 1024
        ),
        cost_estimate=pl.CostEstimate(flops=int(14e9), transcendentals=int(3e6), bytes_accessed=int(46e6)),
        name="attend_backward",
    )(q, k, v, og, ctx, res, doc_col, doc_row, weight, weight)


def on_device(query_rows, key_rows, value_rows, residual_in, out_grad, doc_ids, out_weight, momentum, step_index):
    q, k, v = query_rows[0], key_rows[0], value_rows[0]
    og = out_grad[0]
    shard = out_weight[0]
    y = lax.axis_index(AY)
    other = swapped(shard, AY, 0)
    both = jnp.concatenate([jnp.where(y == 0, shard, other), jnp.where(y == 0, other, shard)], axis=0)
    doc_col = jnp.broadcast_to(doc_ids[0][:, None], (TOK, HEAD_SIZE))
    doc_row = jnp.broadcast_to(doc_ids, (8, TOK))
    some = forward_pass(q, k, v, og, doc_col, doc_row, 0, 2)
    *some, both = lax.optimization_barrier((*some, both))
    weight = lax.all_gather(both, (AX, AZ), tiled=True)
    context, term = forward_pass(q, k, v, og, doc_col, doc_row, 2, 2, some)
    pair = lax.psum_scatter(term, (AX, AZ), scatter_dimension=0, tiled=True)
    block_out, query_grad, key_grad, value_grad = backward_pass(
        q, k, v, og, context, residual_in[0], doc_col, doc_row, weight
    )
    pair, query_grad = lax.optimization_barrier((pair, query_grad))
    sent = jnp.where(y == 0, pair[SHARD:], pair[:SHARD])
    kept = jnp.where(y == 0, pair[:SHARD], pair[SHARD:])
    weight_grad = kept.astype(f32) + swapped(sent, AY, 0).astype(f32)
    new_momentum = momentum_decay * momentum[0] + weight_grad
    stepped = (shard.astype(f32) - learning_rate * new_momentum).astype(bf16)
    levels = lax.axis_size("rep").bit_length() - 1
    branches = [functools.partial(swapped, axis="rep", distance=level) for level in range(levels)]
    partner = lax.switch(step_index[0] % levels, branches, stepped)
    new_weight = ((stepped.astype(f32) + partner.astype(f32)) * 0.5).astype(bf16)
    return (
        block_out[None],
        query_grad[None],
        key_grad[None],
        value_grad[None],
        new_weight[None],
        new_momentum[None],
    )


def solution(mesh):
    torus = Mesh(mesh.devices.reshape(mesh.shape["rep"], 4, 4, 2), ("rep", AX, AZ, AY))
    rows = P("rep", FSDP, None)
    return jax.shard_map(
        on_device,
        mesh=torus,
        in_specs=(rows, rows, rows, rows, rows, P("rep", FSDP), rows, rows, P()),
        out_specs=(rows,) * 6,
        check_vma=False,
    )
```

```python
import functools

import jax
import jax.numpy as jnp
from jax import lax
from jax.experimental import pallas as pl
from jax.experimental.pallas import tpu as pltpu
from jax.sharding import Mesh
from jax.sharding import PartitionSpec as P

HEADS = 20
HEAD_SIZE = 128
TOK = 384
WIDTH = 2560
SHARD = 80
AX, AZ, AY = "fsdp_0", "fsdp_1", "fsdp_2"
FSDP = (AX, AZ, AY)

momentum_decay = 0.9
learning_rate = 0.0003
score_scale = HEAD_SIZE ** (-0.5)

FORWARD_HEADS = 5
BACKWARD_HEADS = 2

bf16 = jnp.bfloat16
f32 = jnp.float32


def swapped(block, axis, distance):
    count = lax.axis_size(axis)
    return lax.ppermute(block, axis, [(i, i ^ (1 << distance)) for i in range(count)])


ROWS_A, ROWS_B, ROWS_C = 32, 16, 32
OFF_A, OFF_B, OFF_C = 0, 32, 48

def from_(block, axis, distance):
    count = lax.axis_size(axis)
    return lax.ppermute(block, axis, [(i, (i - distance) % count) for i in range(count)])


def ring_gather(block, axis):
    half = block.shape[0] // 2
    up = from_(block, axis, 1)
    down = from_(block, axis, -1)
    two_low = from_(up[:half], axis, 1)
    two_high = from_(down[half:], axis, -1)
    return up, down, two_low, two_high


def direct_gather(block, axis):
    return jnp.concatenate(
        [block, from_(block, axis, 1), from_(block, axis, 2), from_(block, axis, -1)], axis=0
    )


def gather_first(shard):
    a = shard[OFF_A : OFF_A + ROWS_A][None]
    b = shard[OFF_B : OFF_B + ROWS_B][None]
    c = shard[OFF_C : OFF_C + ROWS_C][None]
    b2 = jnp.concatenate([b, from_(b, AY, 1)], axis=0)
    c2 = jnp.concatenate([c, from_(c, AY, 1)], axis=0)
    return direct_gather(a, AX), b2, c2


def gather_second(a4, b2, c2):
    return direct_gather(b2, AX), direct_gather(c2, AZ), from_(a4, AY, 1)


def gather_last(a4, b8, c8, a4_y):
    parts = []
    order = [(dx, dy) for dx in range(4) for dy in range(2)]
    a_up, a_down, a_low, a_high = ring_gather(a4, AZ)
    up, down, low, high = ring_gather(b8, AZ)
    for array, dz, places in ((b8, 0, order), (up, 1, order), (down, 3, order), (low, 2, order[:4]), (high, 2, order[4:])):
        parts.append((array, OFF_B, [(dx, dz, dy) for dx, dy in places]))
    up, down, low, high = ring_gather(c8, AX)
    for array, dx, places in ((c8, 0, order), (up, 1, order), (down, 3, order), (low, 2, order[:4]), (high, 2, order[4:])):
        parts.append((array, OFF_C, [(dx, dz, dy) for dz, dy in places]))
    mine = [
        (a4, a4_y, [(k, 0) for k in range(4)]),
        (a_up, None, [(k, 1) for k in range(4)]),
        (a_down, None, [(k, 3) for k in range(4)]),
        (a_low, None, [(k, 2) for k in range(2)]),
        (a_high, None, [(k, 2) for k in range(2, 4)]),
    ]
    for array, across, places in mine:
        across = from_(array, AY, 1) if across is None else across
        parts.append((array, OFF_A, [(dx, dz, 0) for dx, dz in places]))
        parts.append((across, OFF_A, [(dx, dz, 1) for dx, dz in places]))
    return parts


def dot(a, b, dims):
    return lax.dot_general(a, b, (dims, ((), ())), preferred_element_type=f32)


def mask_bias(doc_col, doc_row):
    rows = lax.broadcasted_iota(jnp.int32, (TOK, TOK), 0)
    cols = lax.broadcasted_iota(jnp.int32, (TOK, TOK), 1)
    allowed = (cols <= rows) & (doc_col == doc_row)
    return jnp.where(allowed, 0.0, -1e30).astype(f32)


def softmax_rows(q, k, bias):
    scores = dot(q, k, ((1,), (1,))) * score_scale + bias
    peak = jnp.max(scores, axis=-1, keepdims=True)
    e = jnp.exp(scores - peak)
    return e * (1.0 / jnp.sum(e, axis=-1, keepdims=True))


def forward_kernel(q, k, v, og, doc_col, doc_row, *refs):
    context, term, bias = refs[-3:]

    @pl.when(pl.program_id(0) == 0)
    def _():
        bias[...] = mask_bias(doc_col[:, :1], doc_row[:1, :])

    for h in range(FORWARD_HEADS):
        cols = slice(h * HEAD_SIZE, (h + 1) * HEAD_SIZE)
        probs = softmax_rows(q[:, cols], k[:, cols], bias[...])
        context[:, cols] = dot(probs.astype(bf16), v[:, cols], ((1,), (0,))).astype(bf16)
    term[...] = dot(context[...], og[...], ((0,), (0,))).astype(bf16)


def whole(shape):
    return pl.BlockSpec(shape, lambda i, *_: (0, 0), pipeline_mode=pl.Buffered(1))


def forward_pass(q, k, v, og, doc_col, doc_row, first, count, earlier=()):
    size = FORWARD_HEADS * HEAD_SIZE
    column = pl.BlockSpec((TOK, size), lambda i: (0, i + first))
    return pl.pallas_call(
        forward_kernel,
        out_shape=[jax.ShapeDtypeStruct((TOK, WIDTH), bf16), jax.ShapeDtypeStruct((WIDTH, WIDTH), bf16)],
        grid_spec=pltpu.PrefetchScalarGridSpec(
            num_scalar_prefetch=0,
            grid=(count,),
            in_specs=[column, column, column, whole((TOK, WIDTH)), whole((TOK, HEAD_SIZE)), whole((8, TOK))]
            + [pl.BlockSpec(memory_space=pl.ANY)] * len(earlier),
            out_specs=[column, pl.BlockSpec((size, WIDTH), lambda i: (i + first, 0))],
            scratch_shapes=[pltpu.VMEM((TOK, TOK), f32)],
        ),
        input_output_aliases={6 + i: i for i in range(len(earlier))},
        compiler_params=pltpu.CompilerParams(
            dimension_semantics=("arbitrary",), vmem_limit_bytes=60 * 1024 * 1024
        ),
        cost_estimate=pl.CostEstimate(
            flops=int(1.65e9) * count, transcendentals=750000 * count, bytes_accessed=int(6e6) * count
        ),
        name="attend_forward",
    )(q, k, v, og, doc_col, doc_row, *earlier)


PAIR = 2 * HEAD_SIZE


def backward_kernel(places, pos, q, k, v, og, ctx, res, doc_col, doc_row, *refs):
    parts = refs[: len(places)]
    block_out, qg, kg, vg, bias, weight, sems = refs[len(places) :]
    step = pl.program_id(0)

    @pl.when(step == 0)
    def _():
        copies = []
        for part, (off, offsets) in zip(parts, places):
            rows = part.shape[1]
            for slot, (dx, dz, dy) in enumerate(offsets):
                x = (pos[0] + dx) % 4
                z = (pos[1] + dz) % 4
                y = (pos[2] + dy) % 2
                row = pl.multiple_of((x * 8 + z * 2 + y) * SHARD + off, 16)
                copies.append(
                    pltpu.make_async_copy(part.at[slot], weight.at[pl.ds(row, rows), :], sems.at[len(copies)])
                )
        for copy in copies:
            copy.start()
        bias[...] = mask_bias(doc_col[:, :1], doc_row[:1, :])
        for copy in copies:
            copy.wait()

    rows = pl.ds(pl.multiple_of(step * PAIR, PAIR), PAIR)
    cg_pair = dot(og[...], weight[rows, :], ((1,), (1,))).astype(bf16)
    block_out[...] = (res[...].astype(f32) + dot(ctx[...], weight[:, rows], ((1,), (0,)))).astype(bf16)
    for h in range(2):
        cols = slice(h * HEAD_SIZE, (h + 1) * HEAD_SIZE)
        qh, kh, vh, cg = q[:, cols], k[:, cols], v[:, cols], cg_pair[:, cols]
        probs = softmax_rows(qh, kh, bias[...])
        vg[:, cols] = dot(probs.astype(bf16), cg, ((0,), (0,))).astype(bf16)
        pg = dot(cg, vh, ((1,), (1,)))
        delta = jnp.sum(pg * probs, axis=-1, keepdims=True)
        ds = (probs * (pg - delta) * score_scale).astype(bf16)
        qg[:, cols] = dot(ds, kh, ((1,), (0,))).astype(bf16)
        kg[:, cols] = dot(ds, qh, ((0,), (0,))).astype(bf16)


def backward_pass(pos, q, k, v, og, ctx, res, doc_col, doc_row, parts):
    places = [(off, offsets) for _, off, offsets in parts]
    arrays = [array for array, _, _ in parts]
    count = sum(len(offsets) for _, offsets in places)
    column = pl.BlockSpec((TOK, PAIR), lambda i, *_: (0, i))
    return pl.pallas_call(
        functools.partial(backward_kernel, places),
        out_shape=[jax.ShapeDtypeStruct((TOK, WIDTH), bf16)] * 4,
        grid_spec=pltpu.PrefetchScalarGridSpec(
            num_scalar_prefetch=1,
            grid=(HEADS // 2,),
            in_specs=[column, column, column, whole((TOK, WIDTH)), whole((TOK, WIDTH)), column, whole((TOK, HEAD_SIZE)), whole((8, TOK))]
            + [pl.BlockSpec(memory_space=pl.ANY)] * len(arrays),
            out_specs=[column] * 4,
            scratch_shapes=[
                pltpu.VMEM((TOK, TOK), f32),
                pltpu.VMEM((WIDTH, WIDTH), bf16),
                pltpu.SemaphoreType.DMA((count,)),
            ],
        ),
        compiler_params=pltpu.CompilerParams(
            dimension_semantics=("arbitrary",), vmem_limit_bytes=60 * 1024 * 1024
        ),
        cost_estimate=pl.CostEstimate(flops=int(14e9), transcendentals=int(3e6), bytes_accessed=int(35e6)),
        name="attend_backward",
    )(pos, q, k, v, og, ctx, res, doc_col, doc_row, *arrays)


def on_device(query_rows, key_rows, value_rows, residual_in, out_grad, doc_ids, out_weight, momentum, step_index):
    q, k, v = query_rows[0], key_rows[0], value_rows[0]
    og = out_grad[0]
    shard = out_weight[0]
    y = lax.axis_index(AY)
    pos = jnp.stack([lax.axis_index(AX), lax.axis_index(AZ), lax.axis_index(AY)]).astype(jnp.int32)
    doc_col = jnp.broadcast_to(doc_ids[0][:, None], (TOK, HEAD_SIZE))
    doc_row = jnp.broadcast_to(doc_ids, (8, TOK))
    first = gather_first(shard)
    done = forward_pass(q, k, v, og, doc_col, doc_row, 0, 1)
    first, done = lax.optimization_barrier((first, done))
    second = gather_second(*first)
    done = forward_pass(q, k, v, og, doc_col, doc_row, 1, 2, done)
    second, done = lax.optimization_barrier((second, done))
    parts = gather_last(first[0], *second)
    context, term = forward_pass(q, k, v, og, doc_col, doc_row, 3, 1, done)
    pair = lax.psum_scatter(term, (AX, AZ), scatter_dimension=0, tiled=True)
    block_out, query_grad, key_grad, value_grad = backward_pass(
        pos, q, k, v, og, context, residual_in[0], doc_col, doc_row, parts
    )
    pair, query_grad = lax.optimization_barrier((pair, query_grad))
    sent = jnp.where(y == 0, pair[SHARD:], pair[:SHARD])
    kept = jnp.where(y == 0, pair[:SHARD], pair[SHARD:])
    weight_grad = kept.astype(f32) + swapped(sent, AY, 0).astype(f32)
    new_momentum = momentum_decay * momentum[0] + weight_grad
    stepped = (shard.astype(f32) - learning_rate * new_momentum).astype(bf16)
    levels = lax.axis_size("rep").bit_length() - 1
    branches = [functools.partial(swapped, axis="rep", distance=level) for level in range(levels)]
    partner = lax.switch(step_index[0] % levels, branches, stepped)
    new_weight = ((stepped.astype(f32) + partner.astype(f32)) * 0.5).astype(bf16)
    return (
        block_out[None],
        query_grad[None],
        key_grad[None],
        value_grad[None],
        new_weight[None],
        new_momentum[None],
    )


def solution(mesh):
    torus = Mesh(mesh.devices.reshape(mesh.shape["rep"], 4, 4, 2), ("rep", AX, AZ, AY))
    rows = P("rep", FSDP, None)
    return jax.shard_map(
        on_device,
        mesh=torus,
        in_specs=(rows, rows, rows, rows, rows, P("rep", FSDP), rows, rows, P()),
        out_specs=(rows,) * 6,
        check_vma=False,
    )
```

```python
import functools

import jax
import jax.numpy as jnp
from jax import lax
from jax.experimental import pallas as pl
from jax.experimental.pallas import tpu as pltpu
from jax.sharding import Mesh
from jax.sharding import PartitionSpec as P

HEADS = 20
HEAD_SIZE = 128
TOK = 384
WIDTH = 2560
SHARD = 80
AX, AZ, AY = "fsdp_0", "fsdp_1", "fsdp_2"
FSDP = (AX, AZ, AY)

momentum_decay = 0.9
learning_rate = 0.0003
score_scale = HEAD_SIZE ** (-0.5)

FORWARD_HEADS = 5
BACKWARD_HEADS = 2

bf16 = jnp.bfloat16
f32 = jnp.float32


def swapped(block, axis, distance):
    count = lax.axis_size(axis)
    return lax.ppermute(block, axis, [(i, i ^ (1 << distance)) for i in range(count)])


ROWS_A, ROWS_B, ROWS_C = 32, 16, 32
OFF_A, OFF_B, OFF_C = 0, 32, 48


def from_(block, axis, distance):
    count = lax.axis_size(axis)
    return lax.ppermute(block, axis, [(i, (i - distance) % count) for i in range(count)])


def ring_gather(block, axis):
    half = block.shape[0] // 2
    up = from_(block, axis, 1)
    down = from_(block, axis, -1)
    two_low = from_(up[:half], axis, 1)
    two_high = from_(down[half:], axis, -1)
    return up, down, two_low, two_high


def long_parts(b8, c8):
    parts = []
    order = [(dx, dy) for dx in range(4) for dy in range(2)]
    c_rest = ring_gather(c8, AX)
    b_rest = ring_gather(b8, AZ)
    slots = ((0, order), (1, order), (3, order), (2, order[:4]), (2, order[4:]))
    for array, (dz, places) in zip((b8, *b_rest), slots):
        parts.append((array, OFF_B, [(dx, dz, dy) for dx, dy in places]))
    for array, (dx, places) in zip((c8, *c_rest), slots):
        parts.append((array, OFF_C, [(dx, dz, dy) for dz, dy in places]))
    return parts


def dot(a, b, dims):
    return lax.dot_general(a, b, (dims, ((), ())), preferred_element_type=f32)


def mask_bias(doc_col, doc_row):
    rows = lax.broadcasted_iota(jnp.int32, (TOK, TOK), 0)
    cols = lax.broadcasted_iota(jnp.int32, (TOK, TOK), 1)
    allowed = (cols <= rows) & (doc_col == doc_row)
    return jnp.where(allowed, 0.0, -1e30).astype(f32)


def softmax_rows(q, k, bias):
    scores = dot(q, k, ((1,), (1,))) * score_scale + bias
    peak = jnp.max(scores, axis=-1, keepdims=True)
    e = jnp.exp(scores - peak)
    return e * (1.0 / jnp.sum(e, axis=-1, keepdims=True))


def forward_kernel(q, k, v, og, doc_col, doc_row, *refs):
    context, term, bias = refs[-3:]

    @pl.when(pl.program_id(0) == 0)
    def _():
        bias[...] = mask_bias(doc_col[:, :1], doc_row[:1, :])

    for h in range(FORWARD_HEADS):
        cols = slice(h * HEAD_SIZE, (h + 1) * HEAD_SIZE)
        probs = softmax_rows(q[:, cols], k[:, cols], bias[...])
        context[:, cols] = dot(probs.astype(bf16), v[:, cols], ((1,), (0,))).astype(bf16)
    term[...] = dot(context[...], og[...], ((0,), (0,))).astype(bf16)


def whole(shape):
    return pl.BlockSpec(shape, lambda i, *_: (0, 0), pipeline_mode=pl.Buffered(1))


def forward_pass(q, k, v, og, doc_col, doc_row, first, count, earlier=()):
    size = FORWARD_HEADS * HEAD_SIZE
    column = pl.BlockSpec((TOK, size), lambda i: (0, i + first))
    return pl.pallas_call(
        forward_kernel,
        out_shape=[jax.ShapeDtypeStruct((TOK, WIDTH), bf16), jax.ShapeDtypeStruct((WIDTH, WIDTH), bf16)],
        grid_spec=pltpu.PrefetchScalarGridSpec(
            num_scalar_prefetch=0,
            grid=(count,),
            in_specs=[column, column, column, whole((TOK, WIDTH)), whole((TOK, HEAD_SIZE)), whole((8, TOK))]
            + [pl.BlockSpec(memory_space=pl.ANY)] * len(earlier),
            out_specs=[column, pl.BlockSpec((size, WIDTH), lambda i: (i + first, 0))],
            scratch_shapes=[pltpu.VMEM((TOK, TOK), f32)],
        ),
        input_output_aliases={6 + i: i for i in range(len(earlier))},
        compiler_params=pltpu.CompilerParams(
            dimension_semantics=("arbitrary",), vmem_limit_bytes=60 * 1024 * 1024
        ),
        cost_estimate=pl.CostEstimate(
            flops=int(1.65e9) * count, transcendentals=750000 * count, bytes_accessed=int(6e6) * count
        ),
        name="attend_forward",
    )(q, k, v, og, doc_col, doc_row, *earlier)


PAIR = 2 * HEAD_SIZE


def backward_kernel(places, pos, q, k, v, og, ctx, res, doc_col, doc_row, *refs):
    parts = refs[: len(places)]
    block_out, qg, kg, vg, bias, weight, sems = refs[len(places) :]
    step = pl.program_id(0)

    @pl.when(step == 0)
    def _():
        copies = []
        for part, (off, offsets) in zip(parts, places):
            rows = part.shape[1]
            for slot, (dx, dz, dy) in enumerate(offsets):
                x = dx if off == OFF_A else (pos[0] + dx) % 4
                z = dz if off == OFF_A else (pos[1] + dz) % 4
                y = (pos[2] + dy) % 2
                row = pl.multiple_of((x * 8 + z * 2 + y) * SHARD + off, 16)
                copies.append(
                    pltpu.make_async_copy(part.at[slot], weight.at[pl.ds(row, rows), :], sems.at[len(copies)])
                )
        for copy in copies:
            copy.start()
        bias[...] = mask_bias(doc_col[:, :1], doc_row[:1, :])
        for copy in copies:
            copy.wait()

    rows = pl.ds(pl.multiple_of(step * PAIR, PAIR), PAIR)
    cg_pair = dot(og[...], weight[rows, :], ((1,), (1,))).astype(bf16)
    block_out[...] = (res[...].astype(f32) + dot(ctx[...], weight[:, rows], ((1,), (0,)))).astype(bf16)
    for h in range(2):
        cols = slice(h * HEAD_SIZE, (h + 1) * HEAD_SIZE)
        qh, kh, vh, cg = q[:, cols], k[:, cols], v[:, cols], cg_pair[:, cols]
        probs = softmax_rows(qh, kh, bias[...])
        vg[:, cols] = dot(probs.astype(bf16), cg, ((0,), (0,))).astype(bf16)
        pg = dot(cg, vh, ((1,), (1,)))
        delta = jnp.sum(pg * probs, axis=-1, keepdims=True)
        ds = (probs * (pg - delta) * score_scale).astype(bf16)
        qg[:, cols] = dot(ds, kh, ((1,), (0,))).astype(bf16)
        kg[:, cols] = dot(ds, qh, ((0,), (0,))).astype(bf16)


def backward_pass(pos, q, k, v, og, ctx, res, doc_col, doc_row, parts):
    places = [(off, offsets) for _, off, offsets in parts]
    arrays = [array for array, _, _ in parts]
    count = sum(len(offsets) for _, offsets in places)
    column = pl.BlockSpec((TOK, PAIR), lambda i, *_: (0, i))
    return pl.pallas_call(
        functools.partial(backward_kernel, places),
        out_shape=[jax.ShapeDtypeStruct((TOK, WIDTH), bf16)] * 4,
        grid_spec=pltpu.PrefetchScalarGridSpec(
            num_scalar_prefetch=1,
            grid=(HEADS // 2,),
            in_specs=[column, column, column, whole((TOK, WIDTH)), whole((TOK, WIDTH)), column, whole((TOK, HEAD_SIZE)), whole((8, TOK))]
            + [pl.BlockSpec(memory_space=pl.ANY)] * len(arrays),
            out_specs=[column] * 4,
            scratch_shapes=[
                pltpu.VMEM((TOK, TOK), f32),
                pltpu.VMEM((WIDTH, WIDTH), bf16),
                pltpu.SemaphoreType.DMA((count,)),
            ],
        ),
        compiler_params=pltpu.CompilerParams(
            dimension_semantics=("arbitrary",), vmem_limit_bytes=60 * 1024 * 1024
        ),
        cost_estimate=pl.CostEstimate(flops=int(14e9), transcendentals=int(3e6), bytes_accessed=int(35e6)),
        name="attend_backward",
    )(pos, q, k, v, og, ctx, res, doc_col, doc_row, *arrays)


def on_device(query_rows, key_rows, value_rows, residual_in, out_grad, doc_ids, out_weight, momentum, step_index):
    q, k, v = query_rows[0], key_rows[0], value_rows[0]
    og = out_grad[0]
    shard = out_weight[0]
    y = lax.axis_index(AY)
    pos = jnp.stack([lax.axis_index(AX), lax.axis_index(AZ), lax.axis_index(AY)]).astype(jnp.int32)
    doc_col = jnp.broadcast_to(doc_ids[0][:, None], (TOK, HEAD_SIZE))
    doc_row = jnp.broadcast_to(doc_ids, (8, TOK))
    a16 = lax.all_gather(shard[OFF_A : OFF_A + ROWS_A], (AX, AZ))
    bc = shard[OFF_B:]
    bc2 = jnp.stack([bc, from_(bc, AY, 1)])
    done = forward_pass(q, k, v, og, doc_col, doc_row, 0, 1)
    bc2, done = lax.optimization_barrier((bc2, done))
    b2, c2 = bc2[:, :ROWS_B], bc2[:, ROWS_B:]
    near = [from_(c2, AZ, 1), from_(c2, AZ, 2), from_(c2, AZ, -1), from_(b2, AX, 1), from_(b2, AX, -1)]
    done = forward_pass(q, k, v, og, doc_col, doc_row, 1, 1, done)
    near, b2, c2, done = lax.optimization_barrier((near, b2, c2, done))
    c8 = jnp.concatenate([c2, *near[:3]], axis=0)
    b8 = jnp.concatenate([b2, near[3], from_(b2, AX, 2), near[4]], axis=0)
    context, term = forward_pass(q, k, v, og, doc_col, doc_row, 2, 2, done)
    places = [(n // 4, n % 4) for n in range(16)]
    parts = [
        (a16, OFF_A, [(dx, dz, 0) for dx, dz in places]),
        (from_(a16, AY, 1), OFF_A, [(dx, dz, 1) for dx, dz in places]),
    ] + long_parts(b8, c8)
    pair = lax.psum_scatter(term, (AX, AZ), scatter_dimension=0, tiled=True)
    block_out, query_grad, key_grad, value_grad = backward_pass(
        pos, q, k, v, og, context, residual_in[0], doc_col, doc_row, parts
    )
    pair, query_grad = lax.optimization_barrier((pair, query_grad))
    sent = jnp.where(y == 0, pair[SHARD:], pair[:SHARD])
    kept = jnp.where(y == 0, pair[:SHARD], pair[SHARD:])
    weight_grad = kept.astype(f32) + swapped(sent, AY, 0).astype(f32)
    new_momentum = momentum_decay * momentum[0] + weight_grad
    stepped = (shard.astype(f32) - learning_rate * new_momentum).astype(bf16)
    levels = lax.axis_size("rep").bit_length() - 1
    branches = [functools.partial(swapped, axis="rep", distance=level) for level in range(levels)]
    partner = lax.switch(step_index[0] % levels, branches, stepped)
    new_weight = ((stepped.astype(f32) + partner.astype(f32)) * 0.5).astype(bf16)
    return (
        block_out[None],
        query_grad[None],
        key_grad[None],
        value_grad[None],
        new_weight[None],
        new_momentum[None],
    )


def solution(mesh):
    torus = Mesh(mesh.devices.reshape(mesh.shape["rep"], 4, 4, 2), ("rep", AX, AZ, AY))
    rows = P("rep", FSDP, None)
    return jax.shard_map(
        on_device,
        mesh=torus,
        in_specs=(rows, rows, rows, rows, rows, P("rep", FSDP), rows, rows, P()),
        out_specs=(rows,) * 6,
        check_vma=False,
    )
```

```python
import functools

import jax
import jax.numpy as jnp
from jax import lax
from jax.experimental import pallas as pl
from jax.experimental.pallas import tpu as pltpu
from jax.sharding import Mesh
from jax.sharding import PartitionSpec as P

HEADS = 20
HEAD_SIZE = 128
TOK = 384
WIDTH = 2560
SHARD = 80
AX, AZ, AY = "fsdp_0", "fsdp_1", "fsdp_2"
FSDP = (AX, AZ, AY)

momentum_decay = 0.9
learning_rate = 0.0003
score_scale = HEAD_SIZE ** (-0.5)

FORWARD_HEADS = 5
BACKWARD_HEADS = 2

bf16 = jnp.bfloat16
f32 = jnp.float32


def swapped(block, axis, distance):
    count = lax.axis_size(axis)
    return lax.ppermute(block, axis, [(i, i ^ (1 << distance)) for i in range(count)])


def from_(block, axis, distance):
    count = lax.axis_size(axis)
    return lax.ppermute(block, axis, [(i, (i - distance) % count) for i in range(count)])


LINKS = {
    "x+": (AX, 1, (1, 0, 0)),
    "x-": (AX, -1, (3, 0, 0)),
    "z+": (AZ, 1, (0, 1, 0)),
    "z-": (AZ, -1, (0, 3, 0)),
    "y": (AY, 1, (0, 0, 1)),
}
SIZES = (4, 4, 2)
ROUNDS = (
    {name: [(place, 0, SHARD)] for name, (_, _, place) in LINKS.items()},
    {
        "x+": [((1, 1, 0), 0, 48), ((1, 3, 0), 0, 80), ((2, 0, 0), 0, 32)],
        "z+": [((1, 1, 0), 48, 80), ((3, 1, 0), 0, 80), ((0, 2, 0), 0, 48)],
        "x-": [((3, 0, 1), 0, 80), ((2, 0, 0), 32, 80), ((3, 3, 0), 0, 32)],
        "z-": [((0, 3, 1), 0, 80), ((0, 2, 0), 48, 80), ((3, 3, 0), 32, 80)],
        "y": [((1, 0, 1), 0, 80), ((0, 1, 1), 0, 80)],
    },
    {
        "x+": [((1, 1, 1), 0, 80), ((1, 2, 0), 0, 80)],
        "x-": [((3, 3, 1), 0, 80), ((3, 2, 0), 0, 80)],
        "z+": [((3, 1, 1), 0, 80), ((2, 1, 0), 0, 80)],
        "z-": [((1, 3, 1), 0, 80), ((2, 3, 0), 0, 80)],
        "y": [((2, 0, 1), 0, 80), ((0, 2, 1), 0, 80)],
    },
    {
        "x+": [((1, 2, 1), 0, 80)],
        "x-": [((3, 2, 1), 0, 80)],
        "z+": [((2, 2, 0), 0, 80)],
        "z-": [((2, 3, 1), 0, 80)],
        "y": [((2, 1, 1), 0, 80)],
    },
    {
        "x+": [((2, 2, 1), 0, 32)],
        "z+": [((2, 2, 1), 32, 48)],
        "y": [((2, 2, 1), 48, 80)],
    },
)


class Held:
    def __init__(self, shard):
        self.arrays = [shard]
        self.segments = [[((0, 0, 0), 0, SHARD, 0)]]

    def rows(self, place, low, high):
        pieces = []
        for array, segments in zip(self.arrays, self.segments):
            for where, first, last, start in segments:
                lo, hi = max(low, first), min(high, last)
                if where == place and lo < hi:
                    pieces.append((lo, array[start + lo - first : start + hi - first]))
        pieces.sort(key=lambda piece: piece[0])
        return [piece for _, piece in pieces]

    def exchange(self, plan):
        got = []
        for name, items in plan.items():
            axis, step, link = LINKS[name]
            pieces, segments, start = [], [], 0
            for place, low, high in items:
                seen_there = tuple((p - l) % n for p, l, n in zip(place, link, SIZES))
                pieces += self.rows(seen_there, low, high)
                segments.append((place, low, high, start))
                start += high - low
            message = pieces[0] if len(pieces) == 1 else jnp.concatenate(pieces, axis=0)
            got.append((from_(message, axis, step), segments))
        for array, segments in got:
            self.arrays.append(array)
            self.segments.append(segments)


def dot(a, b, dims):
    return lax.dot_general(a, b, (dims, ((), ())), preferred_element_type=f32)


def mask_bias(doc_col, doc_row):
    rows = lax.broadcasted_iota(jnp.int32, (TOK, TOK), 0)
    cols = lax.broadcasted_iota(jnp.int32, (TOK, TOK), 1)
    allowed = (cols <= rows) & (doc_col == doc_row)
    return jnp.where(allowed, 0.0, -1e30).astype(f32)


def softmax_rows(q, k, bias):
    scores = dot(q, k, ((1,), (1,))) * score_scale + bias
    peak = jnp.max(scores, axis=-1, keepdims=True)
    e = jnp.exp(scores - peak)
    return e * (1.0 / jnp.sum(e, axis=-1, keepdims=True))


def forward_kernel(q, k, v, og, doc_col, doc_row, *refs):
    context, term, bias = refs[-3:]

    @pl.when(pl.program_id(0) == 0)
    def _():
        bias[...] = mask_bias(doc_col[:, :1], doc_row[:1, :])

    for h in range(FORWARD_HEADS):
        cols = slice(h * HEAD_SIZE, (h + 1) * HEAD_SIZE)
        probs = softmax_rows(q[:, cols], k[:, cols], bias[...])
        context[:, cols] = dot(probs.astype(bf16), v[:, cols], ((1,), (0,))).astype(bf16)
    term[...] = dot(context[...], og[...], ((0,), (0,))).astype(bf16)


def whole(shape):
    return pl.BlockSpec(shape, lambda i, *_: (0, 0), pipeline_mode=pl.Buffered(1))


def forward_pass(q, k, v, og, doc_col, doc_row, first, count, earlier=()):
    size = FORWARD_HEADS * HEAD_SIZE
    column = pl.BlockSpec((TOK, size), lambda i: (0, i + first))
    return pl.pallas_call(
        forward_kernel,
        out_shape=[jax.ShapeDtypeStruct((TOK, WIDTH), bf16), jax.ShapeDtypeStruct((WIDTH, WIDTH), bf16)],
        grid_spec=pltpu.PrefetchScalarGridSpec(
            num_scalar_prefetch=0,
            grid=(count,),
            in_specs=[column, column, column, whole((TOK, WIDTH)), whole((TOK, HEAD_SIZE)), whole((8, TOK))]
            + [pl.BlockSpec(memory_space=pl.ANY)] * len(earlier),
            out_specs=[column, pl.BlockSpec((size, WIDTH), lambda i: (i + first, 0))],
            scratch_shapes=[pltpu.VMEM((TOK, TOK), f32)],
        ),
        input_output_aliases={6 + i: i for i in range(len(earlier))},
        compiler_params=pltpu.CompilerParams(
            dimension_semantics=("arbitrary",), vmem_limit_bytes=60 * 1024 * 1024
        ),
        cost_estimate=pl.CostEstimate(
            flops=int(1.65e9) * count, transcendentals=750000 * count, bytes_accessed=int(6e6) * count
        ),
        name="attend_forward",
    )(q, k, v, og, doc_col, doc_row, *earlier)


PAIR = 2 * HEAD_SIZE


def backward_kernel(places, pos, q, k, v, og, ctx, res, doc_col, doc_row, *refs):
    parts = refs[: len(places)]
    block_out, qg, kg, vg, bias, weight, sems = refs[len(places) :]
    step = pl.program_id(0)

    @pl.when(step == 0)
    def _():
        copies = []
        for part, segments in zip(parts, places):
            for (dx, dz, dy), low, high, start in segments:
                x = (pos[0] + dx) % 4
                z = (pos[1] + dz) % 4
                y = (pos[2] + dy) % 2
                row = pl.multiple_of((x * 8 + z * 2 + y) * SHARD + low, 16)
                copies.append(
                    pltpu.make_async_copy(
                        part.at[pl.ds(start, high - low), :],
                        weight.at[pl.ds(row, high - low), :],
                        sems.at[len(copies)],
                    )
                )
        for copy in copies:
            copy.start()
        bias[...] = mask_bias(doc_col[:, :1], doc_row[:1, :])
        for copy in copies:
            copy.wait()

    rows = pl.ds(pl.multiple_of(step * PAIR, PAIR), PAIR)
    cg_pair = dot(og[...], weight[rows, :], ((1,), (1,))).astype(bf16)
    block_out[...] = (res[...].astype(f32) + dot(ctx[...], weight[:, rows], ((1,), (0,)))).astype(bf16)
    for h in range(2):
        cols = slice(h * HEAD_SIZE, (h + 1) * HEAD_SIZE)
        qh, kh, vh, cg = q[:, cols], k[:, cols], v[:, cols], cg_pair[:, cols]
        probs = softmax_rows(qh, kh, bias[...])
        vg[:, cols] = dot(probs.astype(bf16), cg, ((0,), (0,))).astype(bf16)
        pg = dot(cg, vh, ((1,), (1,)))
        delta = jnp.sum(pg * probs, axis=-1, keepdims=True)
        ds = (probs * (pg - delta) * score_scale).astype(bf16)
        qg[:, cols] = dot(ds, kh, ((1,), (0,))).astype(bf16)
        kg[:, cols] = dot(ds, qh, ((0,), (0,))).astype(bf16)


def backward_pass(pos, q, k, v, og, ctx, res, doc_col, doc_row, arrays, places):
    count = sum(len(segments) for segments in places)
    column = pl.BlockSpec((TOK, PAIR), lambda i, *_: (0, i))
    return pl.pallas_call(
        functools.partial(backward_kernel, places),
        out_shape=[jax.ShapeDtypeStruct((TOK, WIDTH), bf16)] * 4,
        grid_spec=pltpu.PrefetchScalarGridSpec(
            num_scalar_prefetch=1,
            grid=(HEADS // 2,),
            in_specs=[column, column, column, whole((TOK, WIDTH)), whole((TOK, WIDTH)), column, whole((TOK, HEAD_SIZE)), whole((8, TOK))]
            + [pl.BlockSpec(memory_space=pl.ANY)] * len(arrays),
            out_specs=[column] * 4,
            scratch_shapes=[
                pltpu.VMEM((TOK, TOK), f32),
                pltpu.VMEM((WIDTH, WIDTH), bf16),
                pltpu.SemaphoreType.DMA((count,)),
            ],
        ),
        compiler_params=pltpu.CompilerParams(
            dimension_semantics=("arbitrary",), vmem_limit_bytes=60 * 1024 * 1024
        ),
        cost_estimate=pl.CostEstimate(flops=int(14e9), transcendentals=int(3e6), bytes_accessed=int(35e6)),
        name="attend_backward",
    )(pos, q, k, v, og, ctx, res, doc_col, doc_row, *arrays)


def on_device(query_rows, key_rows, value_rows, residual_in, out_grad, doc_ids, out_weight, momentum, step_index):
    q, k, v = query_rows[0], key_rows[0], value_rows[0]
    og = out_grad[0]
    shard = out_weight[0]
    y = lax.axis_index(AY)
    pos = jnp.stack([lax.axis_index(AX), lax.axis_index(AZ), lax.axis_index(AY)]).astype(jnp.int32)
    doc_col = jnp.broadcast_to(doc_ids[0][:, None], (TOK, HEAD_SIZE))
    doc_row = jnp.broadcast_to(doc_ids, (8, TOK))
    held = Held(shard)
    held.exchange(ROUNDS[0])
    done = forward_pass(q, k, v, og, doc_col, doc_row, 0, 1)
    held.arrays, done = lax.optimization_barrier((held.arrays, done))
    held.exchange(ROUNDS[1])
    context, term = forward_pass(q, k, v, og, doc_col, doc_row, 1, 3, done)
    held.arrays, context, term = lax.optimization_barrier((held.arrays, context, term))
    for plan in ROUNDS[2:]:
        held.exchange(plan)
    pair = lax.psum_scatter(term, (AX, AZ), scatter_dimension=0, tiled=True)
    block_out, query_grad, key_grad, value_grad = backward_pass(
        pos, q, k, v, og, context, residual_in[0], doc_col, doc_row, held.arrays, held.segments
    )
    pair, query_grad = lax.optimization_barrier((pair, query_grad))
    sent = jnp.where(y == 0, pair[SHARD:], pair[:SHARD])
    kept = jnp.where(y == 0, pair[:SHARD], pair[SHARD:])
    weight_grad = kept.astype(f32) + swapped(sent, AY, 0).astype(f32)
    new_momentum = momentum_decay * momentum[0] + weight_grad
    stepped = (shard.astype(f32) - learning_rate * new_momentum).astype(bf16)
    levels = lax.axis_size("rep").bit_length() - 1
    branches = [functools.partial(swapped, axis="rep", distance=level) for level in range(levels)]
    partner = lax.switch(step_index[0] % levels, branches, stepped)
    new_weight = ((stepped.astype(f32) + partner.astype(f32)) * 0.5).astype(bf16)
    return (
        block_out[None],
        query_grad[None],
        key_grad[None],
        value_grad[None],
        new_weight[None],
        new_momentum[None],
    )


def solution(mesh):
    torus = Mesh(mesh.devices.reshape(mesh.shape["rep"], 4, 4, 2), ("rep", AX, AZ, AY))
    rows = P("rep", FSDP, None)
    return jax.shard_map(
        on_device,
        mesh=torus,
        in_specs=(rows, rows, rows, rows, rows, P("rep", FSDP), rows, rows, P()),
        out_specs=(rows,) * 6,
        check_vma=False,
    )
```

```python
import functools

import jax
import jax.numpy as jnp
from jax import lax
from jax.experimental import pallas as pl
from jax.experimental.pallas import tpu as pltpu
from jax.sharding import Mesh
from jax.sharding import PartitionSpec as P

HEADS = 20
HEAD_SIZE = 128
TOK = 384
WIDTH = 2560
SHARD = 80
AX, AZ, AY = "fsdp_0", "fsdp_1", "fsdp_2"
FSDP = (AX, AZ, AY)

momentum_decay = 0.9
learning_rate = 0.0003
score_scale = HEAD_SIZE ** (-0.5)

FORWARD_HEADS = 5
BACKWARD_HEADS = 2

bf16 = jnp.bfloat16
f32 = jnp.float32


def swapped(block, axis, distance):
    count = lax.axis_size(axis)
    return lax.ppermute(block, axis, [(i, i ^ (1 << distance)) for i in range(count)])


def from_(block, axis, distance):
    count = lax.axis_size(axis)
    return lax.ppermute(block, axis, [(i, (i - distance) % count) for i in range(count)])


LINKS = {
    "x+": (AX, 1, (1, 0, 0)),
    "x-": (AX, -1, (3, 0, 0)),
    "z+": (AZ, 1, (0, 1, 0)),
    "z-": (AZ, -1, (0, 3, 0)),
    "y": (AY, 1, (0, 0, 1)),
}
SIZES = (4, 4, 2)
ROUNDS = (
    {name: [(place, 0, SHARD)] for name, (_, _, place) in LINKS.items()},
    {
        "x+": [((1, 1, 0), 0, 48), ((1, 3, 0), 0, 80), ((2, 0, 0), 0, 32)],
        "z+": [((1, 1, 0), 48, 80), ((3, 1, 0), 0, 80), ((0, 2, 0), 0, 48)],
        "x-": [((3, 0, 1), 0, 80), ((2, 0, 0), 32, 80), ((3, 3, 0), 0, 32)],
        "z-": [((0, 3, 1), 0, 80), ((0, 2, 0), 48, 80), ((3, 3, 0), 32, 80)],
        "y": [((1, 0, 1), 0, 80), ((0, 1, 1), 0, 80)],
    },
    {
        "x+": [((1, 2, 0), 0, 80), ((1, 3, 1), 0, 48)],
        "x-": [((3, 2, 0), 0, 80), ((3, 1, 1), 0, 32)],
        "z+": [((2, 1, 0), 0, 80), ((3, 1, 1), 32, 80)],
        "z-": [((2, 3, 0), 0, 80), ((1, 3, 1), 48, 80)],
        "y": [((2, 0, 1), 0, 80), ((0, 2, 1), 0, 80), ((1, 1, 1), 0, 80), ((3, 3, 1), 0, 80)],
    },
    {
        "x+": [((2, 2, 0), 0, 32)],
        "x-": [((3, 2, 1), 0, 80)],
        "z+": [((2, 2, 0), 32, 80)],
        "z-": [((2, 3, 1), 0, 80)],
        "y": [((2, 1, 1), 0, 80), ((1, 2, 1), 0, 80)],
    },
    {
        "x+": [((2, 2, 1), 0, 32)],
        "y": [((2, 2, 1), 32, 80)],
    },
)


class Held:
    def __init__(self, shard):
        self.arrays = [shard]
        self.segments = [[((0, 0, 0), 0, SHARD, 0)]]

    def rows(self, place, low, high):
        pieces = []
        for array, segments in zip(self.arrays, self.segments):
            for where, first, last, start in segments:
                lo, hi = max(low, first), min(high, last)
                if where == place and lo < hi:
                    pieces.append((lo, array[start + lo - first : start + hi - first]))
        pieces.sort(key=lambda piece: piece[0])
        return [piece for _, piece in pieces]

    def exchange(self, plan):
        got = []
        for name, items in plan.items():
            axis, step, link = LINKS[name]
            pieces, segments, start = [], [], 0
            for place, low, high in items:
                seen_there = tuple((p - l) % n for p, l, n in zip(place, link, SIZES))
                pieces += self.rows(seen_there, low, high)
                segments.append((place, low, high, start))
                start += high - low
            message = pieces[0] if len(pieces) == 1 else jnp.concatenate(pieces, axis=0)
            got.append((from_(message, axis, step), segments))
        for array, segments in got:
            self.arrays.append(array)
            self.segments.append(segments)


def dot(a, b, dims):
    return lax.dot_general(a, b, (dims, ((), ())), preferred_element_type=f32)


def mask_bias(doc_col, doc_row):
    rows = lax.broadcasted_iota(jnp.int32, (TOK, TOK), 0)
    cols = lax.broadcasted_iota(jnp.int32, (TOK, TOK), 1)
    allowed = (cols <= rows) & (doc_col == doc_row)
    return jnp.where(allowed, 0.0, -1e30).astype(f32)


def softmax_rows(q, k, bias):
    scores = dot(q, k, ((1,), (1,))) * score_scale + bias
    peak = jnp.max(scores, axis=-1, keepdims=True)
    e = jnp.exp(scores - peak)
    return e * (1.0 / jnp.sum(e, axis=-1, keepdims=True))


def forward_kernel(q, k, v, og, doc_col, doc_row, *refs):
    context, term, kept_probs, bias = refs[-4:]

    @pl.when(pl.program_id(0) == 0)
    def _():
        bias[...] = mask_bias(doc_col[:, :1], doc_row[:1, :])

    for h in range(FORWARD_HEADS):
        cols = slice(h * HEAD_SIZE, (h + 1) * HEAD_SIZE)
        probs = softmax_rows(q[:, cols], k[:, cols], bias[...]).astype(bf16)
        kept_probs[h] = probs
        context[:, cols] = dot(probs, v[:, cols], ((1,), (0,))).astype(bf16)
    term[...] = dot(context[...], og[...], ((0,), (0,))).astype(bf16)


def whole(shape):
    return pl.BlockSpec(shape, lambda i, *_: (0, 0), pipeline_mode=pl.Buffered(1))


def forward_pass(q, k, v, og, doc_col, doc_row, first, count, earlier=()):
    size = FORWARD_HEADS * HEAD_SIZE
    column = pl.BlockSpec((TOK, size), lambda i: (0, i + first))
    return pl.pallas_call(
        forward_kernel,
        out_shape=[
            jax.ShapeDtypeStruct((TOK, WIDTH), bf16),
            jax.ShapeDtypeStruct((WIDTH, WIDTH), bf16),
            jax.ShapeDtypeStruct((HEADS, TOK, TOK), bf16),
        ],
        grid_spec=pltpu.PrefetchScalarGridSpec(
            num_scalar_prefetch=0,
            grid=(count,),
            in_specs=[column, column, column, whole((TOK, WIDTH)), whole((TOK, HEAD_SIZE)), whole((8, TOK))]
            + [pl.BlockSpec(memory_space=pl.ANY)] * len(earlier),
            out_specs=[
                column,
                pl.BlockSpec((size, WIDTH), lambda i: (i + first, 0)),
                pl.BlockSpec((FORWARD_HEADS, TOK, TOK), lambda i: (i + first, 0, 0)),
            ],
            scratch_shapes=[pltpu.VMEM((TOK, TOK), f32)],
        ),
        input_output_aliases={6 + i: i for i in range(len(earlier))},
        compiler_params=pltpu.CompilerParams(
            dimension_semantics=("arbitrary",), vmem_limit_bytes=60 * 1024 * 1024
        ),
        cost_estimate=pl.CostEstimate(
            flops=int(1.65e9) * count, transcendentals=750000 * count, bytes_accessed=int(6e6) * count
        ),
        name="attend_forward",
    )(q, k, v, og, doc_col, doc_row, *earlier)


PAIR = 2 * HEAD_SIZE
PAIRS = HEADS // 2
OUT_COLS = 512


def backward_kernel(places, pos, q, k, v, probs, og, ctx, res, *refs):
    parts = refs[: len(places)]
    block_out, qg, kg, vg, weight, sems = refs[len(places) :]
    step = pl.program_id(0)

    @pl.when(step == 0)
    def _():
        for part, segments in zip(parts, places):
            for (dx, dz, dy), low, high, start in segments:
                x = (pos[0] + dx) % 4
                z = (pos[1] + dz) % 4
                y = (pos[2] + dy) % 2
                shard = x * 8 + z * 2 + y
                row = pl.multiple_of(shard * SHARD + low, 16)
                pltpu.make_async_copy(
                    part.at[pl.ds(start, high - low), :], weight.at[pl.ds(row, high - low), :], sems.at[shard]
                ).start()

    seen = 0
    for i in range(PAIRS):
        need = min(((i + 1) * PAIR - 1) // SHARD + 1, WIDTH // SHARD)

        @pl.when(step == i)
        def _():
            for shard in range(seen, need):
                whole_shard = weight.at[pl.ds(shard * SHARD, SHARD), :]
                pltpu.make_async_copy(whole_shard, whole_shard, sems.at[shard]).wait()

        seen = need

    @pl.when(step < PAIRS)
    def _():
        rows = pl.ds(pl.multiple_of(step * PAIR, PAIR), PAIR)
        cg_pair = dot(og[...], weight[rows, :], ((1,), (1,))).astype(bf16)
        for h in range(2):
            cols = slice(h * HEAD_SIZE, (h + 1) * HEAD_SIZE)
            qh, kh, vh, cg, p = q[:, cols], k[:, cols], v[:, cols], cg_pair[:, cols], probs[h]
            vg[:, cols] = dot(p, cg, ((0,), (0,))).astype(bf16)
            pg = dot(cg, vh, ((1,), (1,)))
            p = p.astype(f32)
            delta = jnp.sum(pg * p, axis=-1, keepdims=True)
            ds = (p * (pg - delta) * score_scale).astype(bf16)
            qg[:, cols] = dot(ds, kh, ((1,), (0,))).astype(bf16)
            kg[:, cols] = dot(ds, qh, ((0,), (0,))).astype(bf16)

    @pl.when(step >= PAIRS)
    def _():
        cols = pl.ds(pl.multiple_of((step - PAIRS) * OUT_COLS, OUT_COLS), OUT_COLS)
        block_out[...] = (res[...].astype(f32) + dot(ctx[...], weight[:, cols], ((1,), (0,)))).astype(bf16)


def backward_pass(pos, q, k, v, probs, og, ctx, res, arrays, places):
    pair = pl.BlockSpec((TOK, PAIR), lambda i, pos: (0, jnp.minimum(i, PAIRS - 1)))
    out = pl.BlockSpec((TOK, OUT_COLS), lambda i, pos: (0, jnp.maximum(i - PAIRS, 0)))
    return pl.pallas_call(
        functools.partial(backward_kernel, places),
        out_shape=[jax.ShapeDtypeStruct((TOK, WIDTH), bf16)] * 4,
        grid_spec=pltpu.PrefetchScalarGridSpec(
            num_scalar_prefetch=1,
            grid=(PAIRS + WIDTH // OUT_COLS,),
            in_specs=[pair, pair, pair]
            + [pl.BlockSpec((2, TOK, TOK), lambda i, pos: (jnp.minimum(i, PAIRS - 1), 0, 0))]
            + [whole((TOK, WIDTH)), whole((TOK, WIDTH)), out]
            + [pl.BlockSpec(memory_space=pl.ANY)] * len(arrays),
            out_specs=[out, pair, pair, pair],
            scratch_shapes=[pltpu.VMEM((WIDTH, WIDTH), bf16), pltpu.SemaphoreType.DMA((WIDTH // SHARD,))],
        ),
        compiler_params=pltpu.CompilerParams(
            dimension_semantics=("arbitrary",), vmem_limit_bytes=60 * 1024 * 1024
        ),
        cost_estimate=pl.CostEstimate(flops=int(14e9), transcendentals=0, bytes_accessed=int(40e6)),
        name="attend_backward",
    )(pos, q, k, v, probs, og, ctx, res, *arrays)


def on_device(query_rows, key_rows, value_rows, residual_in, out_grad, doc_ids, out_weight, momentum, step_index):
    q, k, v = query_rows[0], key_rows[0], value_rows[0]
    og = out_grad[0]
    shard = out_weight[0]
    y = lax.axis_index(AY)
    pos = jnp.stack([lax.axis_index(AX), lax.axis_index(AZ), lax.axis_index(AY)]).astype(jnp.int32)
    doc_col = jnp.broadcast_to(doc_ids[0][:, None], (TOK, HEAD_SIZE))
    doc_row = jnp.broadcast_to(doc_ids, (8, TOK))
    held = Held(shard)
    held.exchange(ROUNDS[0])
    done = forward_pass(q, k, v, og, doc_col, doc_row, 0, 1)
    held.arrays, done = lax.optimization_barrier((held.arrays, done))
    held.exchange(ROUNDS[1])
    done = forward_pass(q, k, v, og, doc_col, doc_row, 1, 3, done)
    held.arrays, (context, term, probs) = lax.optimization_barrier((held.arrays, done))
    for plan in ROUNDS[2:]:
        held.exchange(plan)
    pair = lax.psum_scatter(term, (AX, AZ), scatter_dimension=0, tiled=True)
    block_out, query_grad, key_grad, value_grad = backward_pass(
        pos, q, k, v, probs, og, context, residual_in[0], held.arrays, held.segments
    )
    pair, query_grad = lax.optimization_barrier((pair, query_grad))
    sent = jnp.where(y == 0, pair[SHARD:], pair[:SHARD])
    kept = jnp.where(y == 0, pair[:SHARD], pair[SHARD:])
    weight_grad = kept.astype(f32) + swapped(sent, AY, 0).astype(f32)
    new_momentum = momentum_decay * momentum[0] + weight_grad
    stepped = (shard.astype(f32) - learning_rate * new_momentum).astype(bf16)
    levels = lax.axis_size("rep").bit_length() - 1
    branches = [functools.partial(swapped, axis="rep", distance=level) for level in range(levels)]
    partner = lax.switch(step_index[0] % levels, branches, stepped)
    new_weight = ((stepped.astype(f32) + partner.astype(f32)) * 0.5).astype(bf16)
    return (
        block_out[None],
        query_grad[None],
        key_grad[None],
        value_grad[None],
        new_weight[None],
        new_momentum[None],
    )


def solution(mesh):
    torus = Mesh(mesh.devices.reshape(mesh.shape["rep"], 4, 4, 2), ("rep", AX, AZ, AY))
    rows = P("rep", FSDP, None)
    return jax.shard_map(
        on_device,
        mesh=torus,
        in_specs=(rows, rows, rows, rows, rows, P("rep", FSDP), rows, rows, P()),
        out_specs=(rows,) * 6,
        check_vma=False,
    )
```

```python
import functools
import math

import jax
import jax.numpy as jnp
from jax import lax
from jax.experimental import pallas as pl
from jax.experimental.pallas import tpu as pltpu
from jax.sharding import Mesh
from jax.sharding import PartitionSpec as P

HEADS = 20
HEAD_SIZE = 128
TOK = 384
WIDTH = 2560
SHARD = 80
AX, AZ, AY = "fsdp_0", "fsdp_1", "fsdp_2"
FSDP = (AX, AZ, AY)

momentum_decay = 0.9
learning_rate = 0.0003
score_scale = HEAD_SIZE ** (-0.5)
LOG2_E = math.log2(math.e)

FORWARD_HEADS = 5
BACKWARD_HEADS = 4

bf16 = jnp.bfloat16
f32 = jnp.float32


def swapped(block, axis, distance):
    count = lax.axis_size(axis)
    return lax.ppermute(block, axis, [(i, i ^ (1 << distance)) for i in range(count)])


def from_(block, axis, distance):
    count = lax.axis_size(axis)
    return lax.ppermute(block, axis, [(i, (i - distance) % count) for i in range(count)])


LINKS = {
    "x+": (AX, 1, (1, 0, 0)),
    "x-": (AX, -1, (3, 0, 0)),
    "z+": (AZ, 1, (0, 1, 0)),
    "z-": (AZ, -1, (0, 3, 0)),
    "y": (AY, 1, (0, 0, 1)),
}
SIZES = (4, 4, 2)
ROUNDS = (
    {name: [(place, 0, SHARD)] for name, (_, _, place) in LINKS.items()},
    {
        "x+": [((1, 1, 0), 0, 48), ((1, 3, 0), 0, 80), ((2, 0, 0), 0, 32)],
        "z+": [((1, 1, 0), 48, 80), ((3, 1, 0), 0, 80), ((0, 2, 0), 0, 48)],
        "x-": [((3, 0, 1), 0, 80), ((2, 0, 0), 32, 80), ((3, 3, 0), 0, 32)],
        "z-": [((0, 3, 1), 0, 80), ((0, 2, 0), 48, 80), ((3, 3, 0), 32, 80)],
        "y": [((1, 0, 1), 0, 80), ((0, 1, 1), 0, 80)],
    },
    {
        "x+": [((1, 1, 1), 0, 80), ((1, 2, 0), 0, 80)],
        "x-": [((3, 3, 1), 0, 80), ((3, 2, 0), 0, 80)],
        "z+": [((3, 1, 1), 0, 80), ((2, 1, 0), 0, 80)],
        "z-": [((1, 3, 1), 0, 80), ((2, 3, 0), 0, 80)],
        "y": [((2, 0, 1), 0, 80), ((0, 2, 1), 0, 80)],
    },
    {
        "x+": [((1, 2, 1), 0, 80)],
        "x-": [((3, 2, 1), 0, 80)],
        "z+": [((2, 2, 0), 0, 80)],
        "z-": [((2, 3, 1), 0, 80)],
        "y": [((2, 1, 1), 0, 80)],
    },
    {
        "x+": [((2, 2, 1), 0, 32)],
        "z+": [((2, 2, 1), 32, 48)],
        "y": [((2, 2, 1), 48, 80)],
    },
)


class Held:
    def __init__(self, shard):
        self.arrays = [shard]
        self.segments = [[((0, 0, 0), 0, SHARD, 0)]]

    def rows(self, place, low, high):
        pieces = []
        for array, segments in zip(self.arrays, self.segments):
            for where, first, last, start in segments:
                lo, hi = max(low, first), min(high, last)
                if where == place and lo < hi:
                    pieces.append((lo, array[start + lo - first : start + hi - first]))
        pieces.sort(key=lambda piece: piece[0])
        return [piece for _, piece in pieces]

    def exchange(self, plan):
        got = []
        for name, items in plan.items():
            axis, step, link = LINKS[name]
            pieces, segments, start = [], [], 0
            for place, low, high in items:
                seen_there = tuple((p - l) % n for p, l, n in zip(place, link, SIZES))
                pieces += self.rows(seen_there, low, high)
                segments.append((place, low, high, start))
                start += high - low
            message = pieces[0] if len(pieces) == 1 else jnp.concatenate(pieces, axis=0)
            got.append((from_(message, axis, step), segments))
        for array, segments in got:
            self.arrays.append(array)
            self.segments.append(segments)


def dot(a, b, dims):
    return lax.dot_general(a, b, (dims, ((), ())), preferred_element_type=f32)


def mask_bias(doc_ids):
    doc_row = jnp.broadcast_to(doc_ids.astype(f32), (TOK, TOK))
    doc_col = doc_row.T
    rows = lax.broadcasted_iota(jnp.int32, (TOK, TOK), 0)
    cols = lax.broadcasted_iota(jnp.int32, (TOK, TOK), 1)
    allowed = (cols <= rows) & (doc_col == doc_row)
    return jnp.where(allowed, 0.0, -1e30).astype(f32)


def softmax_exponents(q, k, bias):
    scores = dot(q, k, ((1,), (1,))) * (score_scale * LOG2_E) + bias
    return jnp.exp2(scores - jnp.max(scores, axis=-1, keepdims=True))


def forward_kernel(q, k, v, og, docs, *refs):
    context, term, kept, bias, valued = refs[-5:]

    @pl.when(pl.program_id(0) == 0)
    def _():
        bias[...] = mask_bias(docs[...])

        valued[:, :, HEAD_SIZE:] = jnp.ones((2, TOK, HEAD_SIZE), bf16)

    for h in range(FORWARD_HEADS):
        cols = slice(h * HEAD_SIZE, (h + 1) * HEAD_SIZE)
        valued[h % 2, :, :HEAD_SIZE] = v[:, cols]
        exponents = softmax_exponents(q[:, cols], k[:, cols], bias[...]).astype(bf16)
        kept[h] = exponents
        sums = dot(exponents, valued[h % 2], ((1,), (0,)))
        context[:, cols] = (sums[:, :HEAD_SIZE] / sums[:, HEAD_SIZE:]).astype(bf16)
    term[...] = dot(context[...], og[...], ((0,), (0,))).astype(bf16)


def whole(shape):
    return pl.BlockSpec(shape, lambda i, *_: (0, 0), pipeline_mode=pl.Buffered(1))


def forward_pass(q, k, v, og, docs, first, count, earlier=()):
    size = FORWARD_HEADS * HEAD_SIZE
    column = pl.BlockSpec((TOK, size), lambda i: (0, i + first))
    return pl.pallas_call(
        forward_kernel,
        out_shape=[
            jax.ShapeDtypeStruct((TOK, WIDTH), bf16),
            jax.ShapeDtypeStruct((WIDTH, WIDTH), bf16),
            jax.ShapeDtypeStruct((HEADS, TOK, TOK), bf16),
        ],
        grid_spec=pltpu.PrefetchScalarGridSpec(
            num_scalar_prefetch=0,
            grid=(count,),
            in_specs=[column, column, column, whole((TOK, WIDTH)), whole((1, TOK))]
            + [pl.BlockSpec(memory_space=pl.ANY)] * len(earlier),
            out_specs=[
                column,
                pl.BlockSpec((size, WIDTH), lambda i: (i + first, 0)),
                pl.BlockSpec((FORWARD_HEADS, TOK, TOK), lambda i: (i + first, 0, 0)),
            ],
            scratch_shapes=[pltpu.VMEM((TOK, TOK), f32), pltpu.VMEM((2, TOK, 2 * HEAD_SIZE), bf16)],
        ),
        input_output_aliases={5 + i: i for i in range(len(earlier))},
        compiler_params=pltpu.CompilerParams(
            dimension_semantics=("arbitrary",), vmem_limit_bytes=60 * 1024 * 1024
        ),
        cost_estimate=pl.CostEstimate(
            flops=int(1.65e9) * count, transcendentals=750000 * count, bytes_accessed=int(6e6) * count
        ),
        name="attend_forward",
    )(q, k, v, og, docs, *earlier)


BACKWARD_COLS = BACKWARD_HEADS * HEAD_SIZE


def backward_kernel(places, pos, q, k, v, kept, og, ctx, res, *refs):
    parts = refs[: len(places)]
    block_out, qg, kg, vg, weight, sems = refs[len(places) :]
    step = pl.program_id(0)

    @pl.when(step == 0)
    def _():
        copies = []
        for part, segments in zip(parts, places):
            for (dx, dz, dy), low, high, start in segments:
                x = (pos[0] + dx) % 4
                z = (pos[1] + dz) % 4
                y = (pos[2] + dy) % 2
                row = pl.multiple_of((x * 8 + z * 2 + y) * SHARD + low, 16)
                copies.append(
                    pltpu.make_async_copy(
                        part.at[pl.ds(start, high - low), :],
                        weight.at[pl.ds(row, high - low), :],
                        sems.at[len(copies)],
                    )
                )
        for copy in copies:
            copy.start()
        for copy in copies:
            copy.wait()

    rows = pl.ds(pl.multiple_of(step * BACKWARD_COLS, BACKWARD_COLS), BACKWARD_COLS)
    cg_all = dot(og[...], weight[rows, :], ((1,), (1,))).astype(bf16)
    block_out[...] = (res[...].astype(f32) + dot(ctx[...], weight[:, rows], ((1,), (0,)))).astype(bf16)
    for h in range(BACKWARD_HEADS):
        cols = slice(h * HEAD_SIZE, (h + 1) * HEAD_SIZE)
        qh, kh, vh, cg = q[:, cols], k[:, cols], v[:, cols], cg_all[:, cols]
        exponents = kept[h].astype(f32)
        probs = exponents * (1.0 / jnp.sum(exponents, axis=-1, keepdims=True))
        vg[:, cols] = dot(probs.astype(bf16), cg, ((0,), (0,))).astype(bf16)
        pg = dot(cg, vh, ((1,), (1,)))
        delta = jnp.sum(pg * probs, axis=-1, keepdims=True)
        ds = (probs * (pg - delta) * score_scale).astype(bf16)
        qg[:, cols] = dot(ds, kh, ((1,), (0,))).astype(bf16)
        kg[:, cols] = dot(ds, qh, ((0,), (0,))).astype(bf16)


def backward_pass(pos, q, k, v, kept, og, ctx, res, arrays, places):
    count = sum(len(segments) for segments in places)
    column = pl.BlockSpec((TOK, BACKWARD_COLS), lambda i, pos: (0, i))
    return pl.pallas_call(
        functools.partial(backward_kernel, places),
        out_shape=[jax.ShapeDtypeStruct((TOK, WIDTH), bf16)] * 4,
        grid_spec=pltpu.PrefetchScalarGridSpec(
            num_scalar_prefetch=1,
            grid=(HEADS // BACKWARD_HEADS,),
            in_specs=[column, column, column, pl.BlockSpec((BACKWARD_HEADS, TOK, TOK), lambda i, pos: (i, 0, 0))]
            + [whole((TOK, WIDTH)), whole((TOK, WIDTH)), column]
            + [pl.BlockSpec(memory_space=pl.ANY)] * len(arrays),
            out_specs=[column] * 4,
            scratch_shapes=[pltpu.VMEM((WIDTH, WIDTH), bf16), pltpu.SemaphoreType.DMA((count,))],
        ),
        compiler_params=pltpu.CompilerParams(
            dimension_semantics=("arbitrary",), vmem_limit_bytes=60 * 1024 * 1024
        ),
        cost_estimate=pl.CostEstimate(flops=int(14e9), transcendentals=0, bytes_accessed=int(40e6)),
        name="attend_backward",
    )(pos, q, k, v, kept, og, ctx, res, *arrays)


def on_device(query_rows, key_rows, value_rows, residual_in, out_grad, doc_ids, out_weight, momentum, step_index):
    q, k, v = query_rows[0], key_rows[0], value_rows[0]
    og = out_grad[0]
    shard = out_weight[0]
    y = lax.axis_index(AY)
    pos = jnp.stack([lax.axis_index(AX), lax.axis_index(AZ), lax.axis_index(AY)]).astype(jnp.int32)
    held = Held(shard)
    held.exchange(ROUNDS[0])
    done = forward_pass(q, k, v, og, doc_ids, 0, 1)
    held.arrays, done = lax.optimization_barrier((held.arrays, done))
    held.exchange(ROUNDS[1])
    done = forward_pass(q, k, v, og, doc_ids, 1, 3, done)
    held.arrays, (context, term, kept) = lax.optimization_barrier((held.arrays, done))
    for plan in ROUNDS[2:]:
        held.exchange(plan)
    pair = lax.psum_scatter(term, (AX, AZ), scatter_dimension=0, tiled=True)
    block_out, query_grad, key_grad, value_grad = backward_pass(
        pos, q, k, v, kept, og, context, residual_in[0], held.arrays, held.segments
    )
    pair, query_grad = lax.optimization_barrier((pair, query_grad))
    own = lax.dynamic_slice_in_dim(pair, y * SHARD, SHARD)
    sent = lax.dynamic_slice_in_dim(pair, (1 - y) * SHARD, SHARD)
    weight_grad = own.astype(f32) + swapped(sent, AY, 0).astype(f32)
    new_momentum = momentum_decay * momentum[0] + weight_grad
    stepped = (shard.astype(f32) - learning_rate * new_momentum).astype(bf16)
    levels = lax.axis_size("rep").bit_length() - 1
    branches = [functools.partial(swapped, axis="rep", distance=level) for level in range(levels)]
    partner = lax.switch(step_index[0] % levels, branches, stepped)
    new_weight = ((stepped.astype(f32) + partner.astype(f32)) * 0.5).astype(bf16)
    return (
        block_out[None],
        query_grad[None],
        key_grad[None],
        value_grad[None],
        new_weight[None],
        new_momentum[None],
    )


def solution(mesh):
    torus = Mesh(mesh.devices.reshape(mesh.shape["rep"], 4, 4, 2), ("rep", AX, AZ, AY))
    rows = P("rep", FSDP, None)
    return jax.shard_map(
        on_device,
        mesh=torus,
        in_specs=(rows, rows, rows, rows, rows, P("rep", FSDP), rows, rows, P()),
        out_specs=(rows,) * 6,
        check_vma=False,
    )
```

```python
import functools
import math

import jax
import jax.numpy as jnp
from jax import lax
from jax.experimental import pallas as pl
from jax.experimental.pallas import tpu as pltpu
from jax.sharding import Mesh
from jax.sharding import PartitionSpec as P

HEADS = 20
HEAD_SIZE = 128
TOK = 384
WIDTH = 2560
SHARD = 80
AX, AZ, AY = "fsdp_0", "fsdp_1", "fsdp_2"
FSDP = (AX, AZ, AY)

momentum_decay = 0.9
learning_rate = 0.0003
score_scale = HEAD_SIZE ** (-0.5)
LOG2_E = math.log2(math.e)

FORWARD_HEADS = 5
BACKWARD_HEADS = 4

bf16 = jnp.bfloat16
f32 = jnp.float32


def swapped(block, axis, distance):
    count = lax.axis_size(axis)
    return lax.ppermute(block, axis, [(i, i ^ (1 << distance)) for i in range(count)])


def from_(block, axis, distance):
    count = lax.axis_size(axis)
    return lax.ppermute(block, axis, [(i, (i - distance) % count) for i in range(count)])


LINKS = {
    "x+": (AX, 1, (1, 0, 0)),
    "x-": (AX, -1, (3, 0, 0)),
    "z+": (AZ, 1, (0, 1, 0)),
    "z-": (AZ, -1, (0, 3, 0)),
    "y": (AY, 1, (0, 0, 1)),
}
SIZES = (4, 4, 2)
ROUNDS = (
    {name: [(place, 0, SHARD)] for name, (_, _, place) in LINKS.items()},
    {
        "x+": [((1, 1, 0), 0, 48), ((1, 3, 0), 0, 80), ((2, 0, 0), 0, 32)],
        "z+": [((1, 1, 0), 48, 80), ((3, 1, 0), 0, 80), ((0, 2, 0), 0, 48)],
        "x-": [((3, 0, 1), 0, 80), ((2, 0, 0), 32, 80), ((3, 3, 0), 0, 32)],
        "z-": [((0, 3, 1), 0, 80), ((0, 2, 0), 48, 80), ((3, 3, 0), 32, 80)],
    },
    {
        "y": [((0, 2, 1), 0, 80), ((2, 0, 1), 0, 80), ((1, 0, 1), 0, 80), ((0, 1, 1), 0, 80), ((1, 1, 1), 0, 80)],
        "x+": [((1, 2, 0), 0, 80), ((1, 3, 1), 0, 80)],
        "z+": [((2, 1, 0), 0, 80), ((3, 1, 1), 0, 80)],
        "x-": [((3, 2, 0), 0, 80), ((3, 3, 1), 0, 32)],
        "z-": [((2, 3, 0), 0, 80), ((3, 3, 1), 32, 80)],
    },
    {
        "x+": [((1, 2, 1), 0, 80)],
        "x-": [((3, 2, 1), 0, 80)],
        "z+": [((2, 2, 0), 0, 80)],
        "z-": [((2, 3, 1), 0, 80)],
        "y": [((2, 1, 1), 0, 80)],
    },
    {
        "x+": [((2, 2, 1), 0, 32)],
        "z+": [((2, 2, 1), 32, 48)],
        "y": [((2, 2, 1), 48, 80)],
    },
)


class Held:
    def __init__(self, shard):
        self.arrays = [shard]
        self.segments = [[((0, 0, 0), 0, SHARD, 0)]]

    def rows(self, place, low, high):
        pieces = []
        for array, segments in zip(self.arrays, self.segments):
            for where, first, last, start in segments:
                lo, hi = max(low, first), min(high, last)
                if where == place and lo < hi:
                    pieces.append((lo, array[start + lo - first : start + hi - first]))
        pieces.sort(key=lambda piece: piece[0])
        return [piece for _, piece in pieces]

    def exchange(self, plan):
        got = []
        for name, items in plan.items():
            axis, step, link = LINKS[name]
            pieces, segments, start = [], [], 0
            for place, low, high in items:
                seen_there = tuple((p - l) % n for p, l, n in zip(place, link, SIZES))
                pieces += self.rows(seen_there, low, high)
                segments.append((place, low, high, start))
                start += high - low
            message = pieces[0] if len(pieces) == 1 else jnp.concatenate(pieces, axis=0)
            got.append((from_(message, axis, step), segments))
        for array, segments in got:
            self.arrays.append(array)
            self.segments.append(segments)


def dot(a, b, dims):
    return lax.dot_general(a, b, (dims, ((), ())), preferred_element_type=f32)


def mask_bias(doc_ids):
    doc_row = jnp.broadcast_to(doc_ids.astype(f32), (TOK, TOK))
    doc_col = doc_row.T
    rows = lax.broadcasted_iota(jnp.int32, (TOK, TOK), 0)
    cols = lax.broadcasted_iota(jnp.int32, (TOK, TOK), 1)
    allowed = (cols <= rows) & (doc_col == doc_row)
    return jnp.where(allowed, 0.0, -1e30).astype(f32)


def softmax_exponents(q, k, bias):
    scores = dot(q, k, ((1,), (1,))) * (score_scale * LOG2_E) + bias
    return jnp.exp2(scores - jnp.max(scores, axis=-1, keepdims=True))


def forward_kernel(q, k, v, og, docs, *refs):
    context, term, kept, bias, valued = refs[-5:]

    @pl.when(pl.program_id(0) == 0)
    def _():
        bias[...] = mask_bias(docs[...])

        valued[:, :, HEAD_SIZE:] = jnp.ones((2, TOK, HEAD_SIZE), bf16)

    for h in range(FORWARD_HEADS):
        cols = slice(h * HEAD_SIZE, (h + 1) * HEAD_SIZE)
        valued[h % 2, :, :HEAD_SIZE] = v[:, cols]
        exponents = softmax_exponents(q[:, cols], k[:, cols], bias[...]).astype(bf16)
        kept[h] = exponents
        sums = dot(exponents, valued[h % 2], ((1,), (0,)))
        context[:, cols] = (sums[:, :HEAD_SIZE] / sums[:, HEAD_SIZE:]).astype(bf16)
    term[...] = dot(context[...], og[...], ((0,), (0,))).astype(bf16)


def whole(shape):
    return pl.BlockSpec(shape, lambda i, *_: (0, 0), pipeline_mode=pl.Buffered(1))


def forward_pass(q, k, v, og, docs, first, count, earlier=()):
    size = FORWARD_HEADS * HEAD_SIZE
    column = pl.BlockSpec((TOK, size), lambda i: (0, i + first))
    return pl.pallas_call(
        forward_kernel,
        out_shape=[
            jax.ShapeDtypeStruct((TOK, WIDTH), bf16),
            jax.ShapeDtypeStruct((WIDTH, WIDTH), bf16),
            jax.ShapeDtypeStruct((HEADS, TOK, TOK), bf16),
        ],
        grid_spec=pltpu.PrefetchScalarGridSpec(
            num_scalar_prefetch=0,
            grid=(count,),
            in_specs=[column, column, column, whole((TOK, WIDTH)), whole((1, TOK))]
            + [pl.BlockSpec(memory_space=pl.ANY)] * len(earlier),
            out_specs=[
                column,
                pl.BlockSpec((size, WIDTH), lambda i: (i + first, 0)),
                pl.BlockSpec((FORWARD_HEADS, TOK, TOK), lambda i: (i + first, 0, 0)),
            ],
            scratch_shapes=[pltpu.VMEM((TOK, TOK), f32), pltpu.VMEM((2, TOK, 2 * HEAD_SIZE), bf16)],
        ),
        input_output_aliases={5 + i: i for i in range(len(earlier))},
        compiler_params=pltpu.CompilerParams(
            dimension_semantics=("arbitrary",), vmem_limit_bytes=60 * 1024 * 1024
        ),
        cost_estimate=pl.CostEstimate(
            flops=int(1.65e9) * count, transcendentals=750000 * count, bytes_accessed=int(6e6) * count
        ),
        name="attend_forward",
    )(q, k, v, og, docs, *earlier)


BACKWARD_COLS = BACKWARD_HEADS * HEAD_SIZE


def backward_kernel(places, pos, q, k, v, kept, og, ctx, res, *refs):
    parts = refs[: len(places)]
    block_out, qg, kg, vg, weight, sems = refs[len(places) :]
    step = pl.program_id(0)

    @pl.when(step == 0)
    def _():
        copies = []
        for part, segments in zip(parts, places):
            for (dx, dz, dy), low, high, start in segments:
                x = (pos[0] + dx) % 4
                z = (pos[1] + dz) % 4
                y = (pos[2] + dy) % 2
                row = pl.multiple_of((x * 8 + z * 2 + y) * SHARD + low, 16)
                copies.append(
                    pltpu.make_async_copy(
                        part.at[pl.ds(start, high - low), :],
                        weight.at[pl.ds(row, high - low), :],
                        sems.at[len(copies)],
                    )
                )
        for copy in copies:
            copy.start()
        for copy in copies:
            copy.wait()

    rows = pl.ds(pl.multiple_of(step * BACKWARD_COLS, BACKWARD_COLS), BACKWARD_COLS)
    cg_all = dot(og[...], weight[rows, :], ((1,), (1,))).astype(bf16)
    block_out[...] = (res[...].astype(f32) + dot(ctx[...], weight[:, rows], ((1,), (0,)))).astype(bf16)
    for h in range(BACKWARD_HEADS):
        cols = slice(h * HEAD_SIZE, (h + 1) * HEAD_SIZE)
        qh, kh, vh, cg = q[:, cols], k[:, cols], v[:, cols], cg_all[:, cols]
        exponents = kept[h].astype(f32)
        probs = exponents * (1.0 / jnp.sum(exponents, axis=-1, keepdims=True))
        vg[:, cols] = dot(probs.astype(bf16), cg, ((0,), (0,))).astype(bf16)
        pg = dot(cg, vh, ((1,), (1,)))
        delta = jnp.sum(pg * probs, axis=-1, keepdims=True)
        ds = (probs * (pg - delta) * score_scale).astype(bf16)
        qg[:, cols] = dot(ds, kh, ((1,), (0,))).astype(bf16)
        kg[:, cols] = dot(ds, qh, ((0,), (0,))).astype(bf16)


def backward_pass(pos, q, k, v, kept, og, ctx, res, arrays, places):
    count = sum(len(segments) for segments in places)
    column = pl.BlockSpec((TOK, BACKWARD_COLS), lambda i, pos: (0, i))
    return pl.pallas_call(
        functools.partial(backward_kernel, places),
        out_shape=[jax.ShapeDtypeStruct((TOK, WIDTH), bf16)] * 4,
        grid_spec=pltpu.PrefetchScalarGridSpec(
            num_scalar_prefetch=1,
            grid=(HEADS // BACKWARD_HEADS,),
            in_specs=[column, column, column, pl.BlockSpec((BACKWARD_HEADS, TOK, TOK), lambda i, pos: (i, 0, 0))]
            + [whole((TOK, WIDTH)), whole((TOK, WIDTH)), column]
            + [pl.BlockSpec(memory_space=pl.ANY)] * len(arrays),
            out_specs=[column] * 4,
            scratch_shapes=[pltpu.VMEM((WIDTH, WIDTH), bf16), pltpu.SemaphoreType.DMA((count,))],
        ),
        compiler_params=pltpu.CompilerParams(
            dimension_semantics=("arbitrary",), vmem_limit_bytes=60 * 1024 * 1024
        ),
        cost_estimate=pl.CostEstimate(flops=int(14e9), transcendentals=0, bytes_accessed=int(40e6)),
        name="attend_backward",
    )(pos, q, k, v, kept, og, ctx, res, *arrays)


def on_device(query_rows, key_rows, value_rows, residual_in, out_grad, doc_ids, out_weight, momentum, step_index):
    q, k, v = query_rows[0], key_rows[0], value_rows[0]
    og = out_grad[0]
    shard = out_weight[0]
    y = lax.axis_index(AY)
    pos = jnp.stack([lax.axis_index(AX), lax.axis_index(AZ), lax.axis_index(AY)]).astype(jnp.int32)
    held = Held(shard)
    held.exchange(ROUNDS[0])
    done = forward_pass(q, k, v, og, doc_ids, 0, 1)
    held.arrays, done = lax.optimization_barrier((held.arrays, done))
    held.exchange(ROUNDS[1])
    done = forward_pass(q, k, v, og, doc_ids, 1, 3, done)
    held.arrays, (context, term, kept) = lax.optimization_barrier((held.arrays, done))
    for plan in ROUNDS[2:]:
        held.exchange(plan)
    pair = lax.psum_scatter(term, (AX, AZ), scatter_dimension=0, tiled=True)
    block_out, query_grad, key_grad, value_grad = backward_pass(
        pos, q, k, v, kept, og, context, residual_in[0], held.arrays, held.segments
    )
    pair, query_grad = lax.optimization_barrier((pair, query_grad))
    own = lax.dynamic_slice_in_dim(pair, y * SHARD, SHARD)
    sent = lax.dynamic_slice_in_dim(pair, (1 - y) * SHARD, SHARD)
    weight_grad = own.astype(f32) + swapped(sent, AY, 0).astype(f32)
    new_momentum = momentum_decay * momentum[0] + weight_grad
    stepped = (shard.astype(f32) - learning_rate * new_momentum).astype(bf16)
    levels = lax.axis_size("rep").bit_length() - 1
    branches = [functools.partial(swapped, axis="rep", distance=level) for level in range(levels)]
    partner = lax.switch(step_index[0] % levels, branches, stepped)
    new_weight = ((stepped.astype(f32) + partner.astype(f32)) * 0.5).astype(bf16)
    return (
        block_out[None],
        query_grad[None],
        key_grad[None],
        value_grad[None],
        new_weight[None],
        new_momentum[None],
    )


def solution(mesh):
    torus = Mesh(mesh.devices.reshape(mesh.shape["rep"], 4, 4, 2), ("rep", AX, AZ, AY))
    rows = P("rep", FSDP, None)
    return jax.shard_map(
        on_device,
        mesh=torus,
        in_specs=(rows, rows, rows, rows, rows, P("rep", FSDP), rows, rows, P()),
        out_specs=(rows,) * 6,
        check_vma=False,
    )
```

```python
import functools
import math

import jax
import jax.numpy as jnp
from jax import lax
from jax.experimental import pallas as pl
from jax.experimental.pallas import tpu as pltpu
from jax.sharding import Mesh
from jax.sharding import PartitionSpec as P

HEADS = 20
HEAD_SIZE = 128
TOK = 384
WIDTH = 2560
SHARD = 80
AX, AZ, AY = "fsdp_0", "fsdp_1", "fsdp_2"
FSDP = (AX, AZ, AY)

momentum_decay = 0.9
learning_rate = 0.0003
score_scale = HEAD_SIZE ** (-0.5)
LOG2_E = math.log2(math.e)

FORWARD_HEADS = 5
BACKWARD_HEADS = 4

bf16 = jnp.bfloat16
f32 = jnp.float32


def swapped(block, axis, distance):
    count = lax.axis_size(axis)
    return lax.ppermute(block, axis, [(i, i ^ (1 << distance)) for i in range(count)])


def from_(block, axis, distance):
    count = lax.axis_size(axis)
    return lax.ppermute(block, axis, [(i, (i - distance) % count) for i in range(count)])


LINKS = {
    "x+": (AX, 1, (1, 0, 0)),
    "x-": (AX, -1, (3, 0, 0)),
    "z+": (AZ, 1, (0, 1, 0)),
    "z-": (AZ, -1, (0, 3, 0)),
    "y": (AY, 1, (0, 0, 1)),
}
SIZES = (4, 4, 2)
ROUNDS = (
    {name: [(place, 0, SHARD)] for name, (_, _, place) in LINKS.items()},
    {
        "x+": [((1, 1, 0), 0, 48), ((1, 3, 0), 0, 80), ((2, 0, 0), 0, 32)],
        "z+": [((1, 1, 0), 48, 80), ((3, 1, 0), 0, 80), ((0, 2, 0), 0, 48)],
        "x-": [((3, 0, 1), 0, 80), ((2, 0, 0), 32, 80), ((3, 3, 0), 0, 32)],
        "z-": [((0, 3, 1), 0, 80), ((0, 2, 0), 48, 80), ((3, 3, 0), 32, 80)],
        "y": [((1, 0, 1), 0, 80), ((0, 1, 1), 0, 80)],
    },
    {
        "x+": [((1, 1, 1), 0, 80), ((1, 2, 0), 0, 80)],
        "x-": [((3, 3, 1), 0, 80), ((3, 2, 0), 0, 80)],
        "z+": [((3, 1, 1), 0, 80), ((2, 1, 0), 0, 80)],
        "z-": [((1, 3, 1), 0, 80), ((2, 3, 0), 0, 80)],
        "y": [((2, 0, 1), 0, 80), ((0, 2, 1), 0, 80)],
    },
    {
        "x+": [((1, 2, 1), 0, 80)],
        "x-": [((3, 2, 1), 0, 80)],
        "z+": [((2, 2, 0), 0, 80)],
        "z-": [((2, 3, 1), 0, 80)],
        "y": [((2, 1, 1), 0, 80)],
    },
    {
        "x+": [((2, 2, 1), 0, 32)],
        "z+": [((2, 2, 1), 32, 48)],
        "y": [((2, 2, 1), 48, 80)],
    },
)


class Held:
    def __init__(self, shard):
        self.arrays = [shard]
        self.segments = [[((0, 0, 0), 0, SHARD, 0)]]

    def rows(self, place, low, high):
        pieces = []
        for array, segments in zip(self.arrays, self.segments):
            for where, first, last, start in segments:
                lo, hi = max(low, first), min(high, last)
                if where == place and lo < hi:
                    pieces.append((lo, array[start + lo - first : start + hi - first]))
        pieces.sort(key=lambda piece: piece[0])
        return [piece for _, piece in pieces]

    def exchange(self, plan):
        got = []
        for name, items in plan.items():
            axis, step, link = LINKS[name]
            pieces, segments, start = [], [], 0
            for place, low, high in items:
                seen_there = tuple((p - l) % n for p, l, n in zip(place, link, SIZES))
                pieces += self.rows(seen_there, low, high)
                segments.append((place, low, high, start))
                start += high - low
            message = pieces[0] if len(pieces) == 1 else jnp.concatenate(pieces, axis=0)
            got.append((from_(message, axis, step), segments))
        for array, segments in got:
            self.arrays.append(array)
            self.segments.append(segments)


def dot(a, b, dims):
    return lax.dot_general(a, b, (dims, ((), ())), preferred_element_type=f32)


def mask_bias(doc_ids):
    doc_row = jnp.broadcast_to(doc_ids.astype(f32), (TOK, TOK))
    doc_col = doc_row.T
    rows = lax.broadcasted_iota(jnp.int32, (TOK, TOK), 0)
    cols = lax.broadcasted_iota(jnp.int32, (TOK, TOK), 1)
    allowed = (cols <= rows) & (doc_col == doc_row)
    return jnp.where(allowed, 0.0, -1e30).astype(f32)


def softmax_exponents(q, k, bias):
    scores = dot(q, k, ((1,), (1,))) * (score_scale * LOG2_E) + bias
    return jnp.exp2(scores - jnp.max(scores, axis=-1, keepdims=True))


def forward_kernel(q, k, v, og, docs, *refs):
    context, term, kept, bias, valued = refs[-5:]

    @pl.when(pl.program_id(0) == 0)
    def _():
        bias[...] = mask_bias(docs[...])

        valued[:, :, HEAD_SIZE:] = jnp.ones((2, TOK, HEAD_SIZE), bf16)

    for h in range(FORWARD_HEADS):
        cols = slice(h * HEAD_SIZE, (h + 1) * HEAD_SIZE)
        valued[h % 2, :, :HEAD_SIZE] = v[:, cols]
        exponents = softmax_exponents(q[:, cols], k[:, cols], bias[...]).astype(bf16)
        kept[h] = exponents
        sums = dot(exponents, valued[h % 2], ((1,), (0,)))
        context[:, cols] = (sums[:, :HEAD_SIZE] / sums[:, HEAD_SIZE:]).astype(bf16)
    term[...] = dot(context[...], og[...], ((0,), (0,))).astype(bf16)


def whole(shape):
    return pl.BlockSpec(shape, lambda i, *_: (0, 0), pipeline_mode=pl.Buffered(1))


def forward_pass(q, k, v, og, docs, first, count, earlier=()):
    size = FORWARD_HEADS * HEAD_SIZE
    column = pl.BlockSpec((TOK, size), lambda i: (0, i + first))
    return pl.pallas_call(
        forward_kernel,
        out_shape=[
            jax.ShapeDtypeStruct((TOK, WIDTH), bf16),
            jax.ShapeDtypeStruct((WIDTH, WIDTH), bf16),
            jax.ShapeDtypeStruct((HEADS, TOK, TOK), bf16),
        ],
        grid_spec=pltpu.PrefetchScalarGridSpec(
            num_scalar_prefetch=0,
            grid=(count,),
            in_specs=[column, column, column, whole((TOK, WIDTH)), whole((1, TOK))]
            + [pl.BlockSpec(memory_space=pl.ANY)] * len(earlier),
            out_specs=[
                column,
                pl.BlockSpec((size, WIDTH), lambda i: (i + first, 0)),
                pl.BlockSpec((FORWARD_HEADS, TOK, TOK), lambda i: (i + first, 0, 0)),
            ],
            scratch_shapes=[pltpu.VMEM((TOK, TOK), f32), pltpu.VMEM((2, TOK, 2 * HEAD_SIZE), bf16)],
        ),
        input_output_aliases={5 + i: i for i in range(len(earlier))},
        compiler_params=pltpu.CompilerParams(
            dimension_semantics=("arbitrary",), vmem_limit_bytes=60 * 1024 * 1024
        ),
        cost_estimate=pl.CostEstimate(
            flops=int(1.65e9) * count, transcendentals=750000 * count, bytes_accessed=int(6e6) * count
        ),
        name="attend_forward",
    )(q, k, v, og, docs, *earlier)


BACKWARD_COLS = BACKWARD_HEADS * HEAD_SIZE


def backward_kernel(places, pos, q, k, v, kept, og, ctx, res, *refs):
    parts = refs[: len(places)]
    block_out, qg, kg, vg, weight, sems = refs[len(places) :]
    step = pl.program_id(0)

    @pl.when(step == 0)
    def _():
        copies = []
        for part, segments in zip(parts, places):
            for (dx, dz, dy), low, high, start in segments:
                x = (pos[0] + dx) % 4
                z = (pos[1] + dz) % 4
                y = (pos[2] + dy) % 2
                row = pl.multiple_of((x * 8 + z * 2 + y) * SHARD + low, 16)
                copies.append(
                    pltpu.make_async_copy(
                        part.at[pl.ds(start, high - low), :],
                        weight.at[pl.ds(row, high - low), :],
                        sems.at[len(copies)],
                    )
                )
        for copy in copies:
            copy.start()
        for copy in copies:
            copy.wait()

    rows = pl.ds(pl.multiple_of(step * BACKWARD_COLS, BACKWARD_COLS), BACKWARD_COLS)
    cg_all = dot(og[...], weight[rows, :], ((1,), (1,))).astype(bf16)
    block_out[...] = (res[...].astype(f32) + dot(ctx[...], weight[:, rows], ((1,), (0,)))).astype(bf16)
    for h in range(BACKWARD_HEADS):
        cols = slice(h * HEAD_SIZE, (h + 1) * HEAD_SIZE)
        qh, kh, vh, cg = q[:, cols], k[:, cols], v[:, cols], cg_all[:, cols]
        exponents = kept[h].astype(f32)
        probs = exponents * (1.0 / jnp.sum(exponents, axis=-1, keepdims=True))
        vg[:, cols] = dot(probs.astype(bf16), cg, ((0,), (0,))).astype(bf16)
        pg = dot(cg, vh, ((1,), (1,)))
        delta = jnp.sum(pg * probs, axis=-1, keepdims=True)
        ds = (probs * (pg - delta) * score_scale).astype(bf16)
        qg[:, cols] = dot(ds, kh, ((1,), (0,))).astype(bf16)
        kg[:, cols] = dot(ds, qh, ((0,), (0,))).astype(bf16)


def backward_pass(pos, q, k, v, kept, og, ctx, res, arrays, places):
    count = sum(len(segments) for segments in places)
    column = pl.BlockSpec((TOK, BACKWARD_COLS), lambda i, pos: (0, i))
    return pl.pallas_call(
        functools.partial(backward_kernel, places),
        out_shape=[jax.ShapeDtypeStruct((TOK, WIDTH), bf16)] * 4,
        grid_spec=pltpu.PrefetchScalarGridSpec(
            num_scalar_prefetch=1,
            grid=(HEADS // BACKWARD_HEADS,),
            in_specs=[column, column, column, pl.BlockSpec((BACKWARD_HEADS, TOK, TOK), lambda i, pos: (i, 0, 0))]
            + [whole((TOK, WIDTH)), whole((TOK, WIDTH)), column]
            + [pl.BlockSpec(memory_space=pl.ANY)] * len(arrays),
            out_specs=[column] * 4,
            scratch_shapes=[pltpu.VMEM((WIDTH, WIDTH), bf16), pltpu.SemaphoreType.DMA((count,))],
        ),
        compiler_params=pltpu.CompilerParams(
            dimension_semantics=("arbitrary",), vmem_limit_bytes=60 * 1024 * 1024
        ),
        cost_estimate=pl.CostEstimate(flops=int(14e9), transcendentals=0, bytes_accessed=int(40e6)),
        name="attend_backward",
    )(pos, q, k, v, kept, og, ctx, res, *arrays)


def on_device(query_rows, key_rows, value_rows, residual_in, out_grad, doc_ids, out_weight, momentum, step_index):
    q, k, v = query_rows[0], key_rows[0], value_rows[0]
    og = out_grad[0]
    shard = out_weight[0]
    y = lax.axis_index(AY)
    pos = jnp.stack([lax.axis_index(AX), lax.axis_index(AZ), lax.axis_index(AY)]).astype(jnp.int32)
    held = Held(shard)
    held.exchange(ROUNDS[0])
    done = forward_pass(q, k, v, og, doc_ids, 0, 1)
    held.arrays, done = lax.optimization_barrier((held.arrays, done))
    held.exchange(ROUNDS[1])
    done = forward_pass(q, k, v, og, doc_ids, 1, 3, done)
    held.arrays, (context, term, kept) = lax.optimization_barrier((held.arrays, done))
    for plan in ROUNDS[2:]:
        held.exchange(plan)
    pair = lax.psum_scatter(term, (AX, AZ), scatter_dimension=0, tiled=True)
    block_out, query_grad, key_grad, value_grad = backward_pass(
        pos, q, k, v, kept, og, context, residual_in[0], held.arrays, held.segments
    )
    pair, query_grad = lax.optimization_barrier((pair, query_grad))
    own = lax.dynamic_slice_in_dim(pair, y * SHARD, SHARD)
    sent = lax.dynamic_slice_in_dim(pair, (1 - y) * SHARD, SHARD)
    other = swapped(sent, AY, 0)
    decayed = momentum_decay * momentum[0]

    def moved(own, other, decayed):
        return decayed + (own.astype(f32) + other.astype(f32))

    def finished(level, stepped, own, other, decayed):
        partner = swapped(stepped, "rep", level)
        new_weight = ((stepped.astype(f32) + partner.astype(f32)) * 0.5).astype(bf16)
        return new_weight, moved(own, other, decayed)

    stepped = (shard.astype(f32) - learning_rate * moved(own, other, decayed)).astype(bf16)
    levels = lax.axis_size("rep").bit_length() - 1
    branches = [functools.partial(finished, level) for level in range(levels)]
    new_weight, new_momentum = lax.switch(step_index[0] % levels, branches, stepped, own, other, decayed)
    return (
        block_out[None],
        query_grad[None],
        key_grad[None],
        value_grad[None],
        new_weight[None],
        new_momentum[None],
    )


def solution(mesh):
    torus = Mesh(mesh.devices.reshape(mesh.shape["rep"], 4, 4, 2), ("rep", AX, AZ, AY))
    rows = P("rep", FSDP, None)
    return jax.shard_map(
        on_device,
        mesh=torus,
        in_specs=(rows, rows, rows, rows, rows, P("rep", FSDP), rows, rows, P()),
        out_specs=(rows,) * 6,
        check_vma=False,
    )
```
